32 devices in a mesh: section: 4 (over y, x), vertex: 4 (over z), feat: 2 (over core).
Axes of the slice: x: 2, y: 2, z: 4, core: 2. Of those that a mesh axis runs over, the one named last changes fastest.
Arguments:
- features: bfloat16 [8192, 1024], P('vertex', 'feat'), may hold values from -6 to 6
- history: bfloat16 [4, 8192, 1024], P('section', 'vertex', 'feat'), may hold values from -6 to 6
- weights: bfloat16 [4, 1024, 1024], P('section', None, 'feat'), may hold values from -0.1875 to 0.1875
- tile_values: bfloat16 [3, 64, 128, 128], P(None, 'vertex'), may hold values from -0.25 to 0.25
- tile_rows: int32 [3, 64], P(None, 'vertex'), may hold values from 0 to 3, as said below
- tile_cols: int32 [3, 64], P(None, 'vertex'), may hold values from 0 to 15
- tile_counts: int32 [3, 4], P(None, 'vertex'), may hold values from 1 to 16, as said below
- span_ids: int32 [3, 512], P(None, 'vertex'), may hold values from 0 to 2047, as said below
Outputs:
- layer_out: bfloat16 [4, 3, 512, 1024], P('section', None, 'vertex', 'feat')
- new_history: bfloat16 [4, 8192, 1024], P('section', 'vertex', 'feat')
The draws below stay inside these ranges and needn't reach their ends.
Inputs may be any that keep to these rules, and one draw needn't show every extreme that they name: `tile_rows`: within one owner's list for one block the (row block, column block) pairs are distinct. `tile_counts`: in every block some owner has exactly 16 live tiles. `span_ids`: the 384 entries of one owner over all blocks are distinct.
All inputs are finite; a program needn't handle non-finite values.
Results may differ from the reference program's by a relative error of at most 0.018.
Values may be sent and summed in bfloat16 or wider, within the bound.
A program may use at most 128 MiB of HBM per device.

```python
import math
import jax
import jax.numpy as jnp
from jax import lax

F = 1024
BLOCK = 128
SPANS = 3
ROWS_DEV = 128
VD = 2048
LAYERS = 4
V = 8192
TILES = 16
N_SECTION = 4
N_VERTEX = 4


def tile_pairs(key):
    row_blocks = ROWS_DEV * N_VERTEX // BLOCK
    col_blocks = VD // BLOCK
    keys = jax.random.split(jax.random.fold_in(key, 11), SPANS * N_VERTEX)
    picks = jax.vmap(lambda single: jax.random.permutation(single, row_blocks * col_blocks)[:TILES])(keys)
    return (picks.reshape(SPANS, N_VERTEX * TILES).astype(jnp.int32), col_blocks)


def draw_tile_rows(key, part):
    picks, col_blocks = tile_pairs(key)
    return (picks // col_blocks).astype(jnp.int32)


def draw_tile_cols(key, part):
    picks, col_blocks = tile_pairs(key)
    return (picks % col_blocks).astype(jnp.int32)


def draw_tile_counts(key, part):
    lowest = max(1, TILES // 8)
    base = jax.random.randint(jax.random.fold_in(key, 5), (SPANS, N_VERTEX), lowest, TILES // 2 + 1)
    busiest = jax.random.randint(jax.random.fold_in(key, 6), (SPANS, 1), 0, N_VERTEX)
    owner_index = jnp.arange(N_VERTEX)[None, :]
    return jnp.where(owner_index == busiest, TILES, base).astype(jnp.int32)


def draw_span_ids(key, part):
    keys = jax.random.split(jax.random.fold_in(key, 17), N_VERTEX)
    picks = jax.vmap(lambda single: jax.random.permutation(single, VD)[:SPANS * ROWS_DEV])(keys)
    picks = picks.reshape(N_VERTEX, SPANS, ROWS_DEV).transpose(1, 0, 2)
    return picks.reshape(SPANS, N_VERTEX * ROWS_DEV).astype(jnp.int32)


def levels(key, shape, shards, least, top_value):
    factor_of, own = 1.0, jax.random.fold_in(key, 6)
    for position, blocks in shards:
        draws = jnp.exp(jax.random.uniform(jax.random.fold_in(own, position), (blocks,), jnp.float32, least / len(shards), top_value / len(shards)))
        factor_of = factor_of * jnp.repeat(draws, shape[position] // blocks).reshape([-1 if axis == position else 1 for axis in range(len(shape))])
    return factor_of


def bell_draw(rng, shape, width, limit, cuts=(), dtype=jnp.bfloat16):
    values = width * jax.random.normal(rng, shape, jnp.float32)
    if cuts:
        values = values * levels(rng, shape, cuts, -0.22, 0.18)
    return jnp.clip(values, -limit, limit).astype(dtype)


def setup_inputs(seed: int = 0) -> dict:
    splits = jax.random.split(jax.random.key(seed), 9)
    features = bell_draw(splits[0], (V, F), 1.0, 6.0, ((0, 4), (1, 2)))
    history = bell_draw(splits[1], (LAYERS, V, F), 1.0, 6.0, ((0, 4), (1, 4), (2, 2)))
    weights = bell_draw(splits[2], (LAYERS, F, F), F ** -0.5, 0.1875, ((0, 4), (2, 2)))
    tile_values = bell_draw(splits[3], (SPANS, N_VERTEX * TILES, BLOCK, BLOCK), (N_VERTEX * VD // 16) ** -0.5, 0.25, ((1, 4),))
    tile_rows = draw_tile_rows(jax.random.fold_in(splits[8], 71), 0)
    tile_cols = draw_tile_cols(jax.random.fold_in(splits[8], 71), 0)
    tile_counts = draw_tile_counts(jax.random.fold_in(splits[8], 71), 0)
    span_ids = draw_span_ids(jax.random.fold_in(splits[8], 71), 0)
    return {"features": features, "history": history, "weights": weights, "tile_values": tile_values, "tile_rows": tile_rows, "tile_cols": tile_cols, "tile_counts": tile_counts, "span_ids": span_ids}


RESIDUAL_SHARE = 0.2
BETA_SCALE = 0.5


def reference(features, history, weights, tile_values, tile_rows, tile_cols, tile_counts, span_ids):
    row_blocks = ROWS_DEV * N_VERTEX // BLOCK
    col_blocks = VD // BLOCK
    owners = (jnp.arange(ROWS_DEV * N_VERTEX) // ROWS_DEV).astype(jnp.int32) * VD
    outputs = []
    tables = []
    previous = None
    for layer in range(N_SECTION):
        table = history[layer]
        beta_rate = math.log(BETA_SCALE / (layer + 1) + 1.0)
        results = []
        for span_index in range(SPANS):
            vertex_ids = span_ids[span_index].astype(jnp.int32) + owners
            initial = features[vertex_ids]
            fresh_rows = initial if layer == 0 else previous[span_index]
            table = table.at[vertex_ids].set(fresh_rows)
            blocks = table.reshape(N_VERTEX * col_blocks, BLOCK, F)
            values_here = tile_values[span_index]
            rows_here = tile_rows[span_index]
            cols_here = tile_cols[span_index]
            counts_here = tile_counts[span_index]

            def device_term(device, running):
                first = (device * TILES).astype(jnp.int32)
                tile_block = lax.dynamic_slice_in_dim(values_here, first, TILES, 0).astype(jnp.float32)
                row_ids = lax.dynamic_slice_in_dim(rows_here, first, TILES, 0)
                col_ids = lax.dynamic_slice_in_dim(cols_here, first, TILES, 0) + (device * col_blocks).astype(jnp.int32)
                alive = (jnp.arange(TILES) < counts_here[device]).astype(jnp.float32)
                picked = blocks[col_ids].astype(jnp.float32)
                products = jnp.einsum("tij,tjc->tic", tile_block, picked, precision=lax.Precision.HIGHEST)
                products = products * alive[:, None, None]
                summed = jax.ops.segment_sum(products, row_ids, num_segments=row_blocks)
                rounded = lax.optimization_barrier(summed.astype(jnp.bfloat16))
                return running + rounded.astype(jnp.float32)

            aggregate = lax.fori_loop(0, N_VERTEX, device_term, jnp.zeros((row_blocks, BLOCK, F), jnp.float32))
            aggregate = aggregate.reshape(ROWS_DEV * N_VERTEX, F)
            support = ((1.0 - RESIDUAL_SHARE) * aggregate + RESIDUAL_SHARE * initial.astype(jnp.float32)).astype(jnp.bfloat16)
            projected = jnp.dot(support, weights[layer], preferred_element_type=jnp.float32)
            layer_rows = jax.nn.relu((1.0 - beta_rate) * support.astype(jnp.float32) + beta_rate * projected).astype(jnp.bfloat16)
            results.append(layer_rows)
        previous = results
        outputs.append(jnp.stack(results))
        tables.append(table)
    return jnp.stack(outputs), jnp.stack(tables)
```

```python
import functools

import jax
import jax.numpy as jnp
from jax import lax
from jax.experimental import pallas as pl
from jax.experimental.pallas import tpu as pltpu
from jax.sharding import PartitionSpec as P

RESIDUAL_SHARE = 0.2
BETA_SCALE = 0.5
MESH = pl.DeviceIdType.MESH
VMEM_BYTES = 60_000 * 1024


def chosen(ids_row, rows, first=0):
    shape = (rows, ids_row.shape[1])
    return (lax.broadcasted_iota(jnp.int32, shape, 0) + first == ids_row).astype(jnp.float32)


def prepare(rows_ref, cols_ref, counts_ref, ids_ref, tiles_ref, table_ref, base_ref, picks_ref, dense, select, kept):
    spans, _, side, _ = tiles_ref.shape
    owned = table_ref.shape[0]
    span_rows = ids_ref.shape[1] // spans
    rows_whole = dense.shape[0]
    chunk = min(256, owned)
    group = min(512, rows_whole)

    for span in range(spans):
        mine = slice(span * span_rows, (span + 1) * span_rows)

        def fill(i, _, span=span, mine=mine):
            first = pl.multiple_of(i * chunk, chunk)
            here = pl.ds(first, chunk)
            hot = chosen(ids_ref[:, mine], chunk, first)
            select[here, mine] = hot.astype(jnp.bfloat16)
            taken = jnp.max(hot, axis=1, keepdims=True)
            source = table_ref if span == 0 else kept
            kept[here, :] = jnp.where(taken > 0.5, 0.0, source[here, :].astype(jnp.float32)).astype(jnp.bfloat16)
            return 0

        lax.fori_loop(0, owned // chunk, fill, 0)
        dense[...] = jnp.zeros_like(dense)

        def place(t, _, span=span):
            row = pl.multiple_of(rows_ref[span, t] * side, side)
            col = pl.multiple_of(cols_ref[span, t] * side, side)
            dense[pl.ds(row, side), pl.ds(col, side)] = tiles_ref[span, t]
            return 0

        lax.fori_loop(0, counts_ref[span, 0], place, 0)
        width = (span + 1) * span_rows

        def multiply(i, _, span=span, width=width):
            here = pl.ds(pl.multiple_of(i * group, group), group)
            block = dense[here, :]
            base_ref[span, here, :] = jnp.dot(block, kept[...], preferred_element_type=jnp.float32)
            picks_ref[span, here, :width] = jnp.dot(
                block, select[:, :width], preferred_element_type=jnp.float32
            ).astype(jnp.bfloat16)
            if width < picks_ref.shape[2]:
                picks_ref[span, here, width:] = jnp.zeros((group, picks_ref.shape[2] - width), jnp.bfloat16)
            return 0

        lax.fori_loop(0, rows_whole // group, multiply, 0)


def relay(
    sections, vertices, feats,
    base_ref, picks_ref, initial_ref, weight_ref, out_ref, fresh_ref,
    arrived, partial, parts, support, other, result,
    x_send, x_recv, p_send, p_recv, s_send, s_recv,
):
    section = lax.axis_index("section")
    vertex = lax.axis_index("vertex")
    feat = lax.axis_index("feat")
    spans, span_rows, width = initial_ref.shape
    rows_whole = base_ref.shape[1]
    group = min(512, rows_whole)
    partner = lax.rem(feat + 1, feats)
    beta = jnp.log(BETA_SCALE / (section + 1).astype(jnp.float32) + 1.0)

    barrier = pltpu.get_barrier_semaphore()
    for step in range(1, vertices):
        peer = lax.rem(vertex + step, vertices)
        pl.semaphore_signal(barrier, inc=1, device_id=(section, peer, feat), device_id_type=MESH)
    pl.semaphore_signal(barrier, inc=1, device_id=(section, vertex, partner), device_id_type=MESH)
    for step in (1, sections - 1):
        peer = lax.rem(section + step, sections)
        pl.semaphore_signal(barrier, inc=1, device_id=(peer, vertex, feat), device_id_type=MESH)
    pl.semaphore_wait(barrier, vertices - 1 + 1 + 2)

    def row_copy(span):
        return pltpu.make_async_remote_copy(
            src_ref=result.at[span], dst_ref=arrived.at[span],
            send_sem=x_send.at[span], recv_sem=x_recv.at[span],
            device_id=(lax.rem(section + 1, sections), vertex, feat), device_id_type=MESH,
        )

    def part_copy(span, step):
        peer = lax.rem(vertex + step, vertices)
        rows = pl.ds(pl.multiple_of(peer * span_rows, span_rows), span_rows)
        return pltpu.make_async_remote_copy(
            src_ref=partial.at[span, rows], dst_ref=parts.at[span, step - 1],
            send_sem=p_send.at[span, step - 1], recv_sem=p_recv.at[span, step - 1],
            device_id=(section, peer, feat), device_id_type=MESH,
        )

    def support_copy(span):
        return pltpu.make_async_remote_copy(
            src_ref=support.at[span], dst_ref=other.at[span],
            send_sem=s_send.at[span], recv_sem=s_recv.at[span],
            device_id=(section, vertex, partner), device_id_type=MESH,
        )

    def scatter(span):
        mine = slice(span * span_rows, (span + 1) * span_rows)

        @pl.when(section == 0)
        def _():
            fresh_ref[mine, :] = initial_ref[span]

        @pl.when(section > 0)
        def _():
            row_copy(span).wait_recv()
            fresh_ref[mine, :] = arrived[span]

        used = (span + 1) * span_rows
        rows_now = fresh_ref[:used, :]

        def add(i, _):
            here = pl.ds(pl.multiple_of(i * group, group), group)
            total = base_ref[span, here, :] + jnp.dot(
                picks_ref[span, here, :used], rows_now, preferred_element_type=jnp.float32
            )
            partial[span, here, :] = total.astype(jnp.bfloat16)
            return 0

        lax.fori_loop(0, rows_whole // group, add, 0)
        for step in range(1, vertices):
            part_copy(span, step).start()

    def finish(span):
        own = pl.ds(pl.multiple_of(vertex * span_rows, span_rows), span_rows)
        total = partial[span, own, :].astype(jnp.float32)
        for step in range(1, vertices):
            part_copy(span, step).wait_recv()
            total += parts[span, step - 1].astype(jnp.float32)
        mixed = (
            (1.0 - RESIDUAL_SHARE) * total + RESIDUAL_SHARE * initial_ref[span].astype(jnp.float32)
        ).astype(jnp.bfloat16)
        support[span] = mixed
        support_copy(span).start()
        mine = pl.ds(pl.multiple_of(feat * width, width), width)
        theirs = pl.ds(pl.multiple_of(partner * width, width), width)
        projected = jnp.dot(mixed, weight_ref[mine, :], preferred_element_type=jnp.float32)
        support_copy(span).wait_recv()
        projected += jnp.dot(other[span], weight_ref[theirs, :], preferred_element_type=jnp.float32)
        rows = jnp.maximum((1.0 - beta) * mixed.astype(jnp.float32) + beta * projected, 0.0).astype(jnp.bfloat16)
        result[span] = rows
        out_ref[span] = rows

        @pl.when(section < sections - 1)
        def _():
            row_copy(span).start()

    scatter(0)
    for span in range(1, spans):
        scatter(span)
        finish(span - 1)
    finish(spans - 1)

    for span in range(spans):
        support_copy(span).wait_send()
        for step in range(1, vertices):
            part_copy(span, step).wait_send()

        @pl.when(section < sections - 1)
        def _(span=span):
            row_copy(span).wait_send()


def merge(ids_ref, table_ref, fresh_ref, out_ref):
    chunk = table_ref.shape[0]
    hot = chosen(ids_ref[...], chunk, pl.program_id(0) * chunk)
    taken = jnp.max(hot, axis=1, keepdims=True)
    moved = jnp.dot(hot.astype(jnp.bfloat16), fresh_ref[...], preferred_element_type=jnp.float32)
    out_ref[...] = jnp.where(taken > 0.5, moved, table_ref[...].astype(jnp.float32)).astype(jnp.bfloat16)


def shards(sizes, features, history, weights, tile_values, tile_rows, tile_cols, tile_counts, span_ids):
    sections, vertices, feats = sizes
    spans, span_rows = span_ids.shape
    side = tile_values.shape[2]
    owned, width = features.shape
    rows_whole = span_rows * vertices
    table = history[0]
    ids_flat = span_ids.reshape(1, spans * span_rows)
    vmem = pl.BlockSpec(memory_space=pltpu.VMEM)
    smem = pl.BlockSpec(memory_space=pltpu.SMEM)
    initial = jnp.take(features, span_ids.reshape(-1), axis=0, mode="clip").reshape(spans, span_rows, width)

    base, picks = pl.pallas_call(
        prepare,
        name="prepare",
        out_shape=(
            jax.ShapeDtypeStruct((spans, rows_whole, width), jnp.float32),
            jax.ShapeDtypeStruct((spans, rows_whole, spans * span_rows), jnp.bfloat16),
        ),
        in_specs=[smem, smem, smem, vmem, vmem, vmem],
        out_specs=(vmem, vmem),
        scratch_shapes=[
            pltpu.VMEM((rows_whole, owned), jnp.bfloat16),
            pltpu.VMEM((owned, spans * span_rows), jnp.bfloat16),
            pltpu.VMEM((owned, width), jnp.bfloat16),
        ],
        compiler_params=pltpu.CompilerParams(vmem_limit_bytes=VMEM_BYTES),
    )(tile_rows, tile_cols, tile_counts, ids_flat, tile_values, table)

    rows_type = jax.ShapeDtypeStruct((spans, span_rows, width), jnp.bfloat16)
    layer_rows, fresh = pl.pallas_call(
        functools.partial(relay, sections, vertices, feats),
        name="relay",
        out_shape=(rows_type, jax.ShapeDtypeStruct((spans * span_rows, width), jnp.bfloat16)),
        in_specs=[vmem] * 4,
        out_specs=(vmem, vmem),
        scratch_shapes=[
            pltpu.VMEM((spans, span_rows, width), jnp.bfloat16),
            pltpu.VMEM((spans, rows_whole, width), jnp.bfloat16),
            pltpu.VMEM((spans, vertices - 1, span_rows, width), jnp.bfloat16),
            pltpu.VMEM((spans, span_rows, width), jnp.bfloat16),
            pltpu.VMEM((spans, span_rows, width), jnp.bfloat16),
            pltpu.VMEM((spans, span_rows, width), jnp.bfloat16),
            pltpu.SemaphoreType.DMA((spans,)),
            pltpu.SemaphoreType.DMA((spans,)),
            pltpu.SemaphoreType.DMA((spans, vertices - 1)),
            pltpu.SemaphoreType.DMA((spans, vertices - 1)),
            pltpu.SemaphoreType.DMA((spans,)),
            pltpu.SemaphoreType.DMA((spans,)),
        ],
        compiler_params=pltpu.CompilerParams(
            vmem_limit_bytes=VMEM_BYTES, collective_id=0, has_side_effects=True
        ),
    )(base, picks, initial, weights[0])

    chunk = min(256, owned)
    table_new = pl.pallas_call(
        merge,
        name="merge",
        grid=(owned // chunk,),
        out_shape=jax.ShapeDtypeStruct((owned, width), jnp.bfloat16),
        in_specs=[
            pl.BlockSpec((1, spans * span_rows), lambda i: (0, 0)),
            pl.BlockSpec((chunk, width), lambda i: (i, 0)),
            pl.BlockSpec((spans * span_rows, width), lambda i: (0, 0)),
        ],
        out_specs=pl.BlockSpec((chunk, width), lambda i: (i, 0)),
    )(ids_flat, table, fresh)
    return (layer_rows[None], table_new[None])


def solution(mesh):
    placed = (
        P("vertex", "feat"),
        P("section", "vertex", "feat"),
        P("section", None, "feat"),
        P(None, "vertex", None, None),
        P(None, "vertex"),
        P(None, "vertex"),
        P(None, "vertex"),
        P(None, "vertex"),
    )
    sizes = (mesh.shape["section"], mesh.shape["vertex"], mesh.shape["feat"])
    return jax.shard_map(
        functools.partial(shards, sizes),
        mesh=mesh,
        in_specs=placed,
        out_specs=(P("section", None, "vertex", "feat"), P("section", "vertex", "feat")),
        check_vma=False,
    )
```

```python
import functools

import jax
import jax.numpy as jnp
from jax import lax
from jax.experimental import pallas as pl
from jax.experimental.pallas import tpu as pltpu
from jax.sharding import PartitionSpec as P

RESIDUAL_SHARE = 0.2
BETA_SCALE = 0.5
MESH = pl.DeviceIdType.MESH
VMEM_BYTES = 60_000 * 1024


def chosen(ids_row, rows, first=0):
    shape = (rows, ids_row.shape[1])
    return (lax.broadcasted_iota(jnp.int32, shape, 0) + first == ids_row).astype(jnp.float32)


def prepare(rows_ref, cols_ref, counts_ref, ids_ref, tiles_ref, table_ref, base_ref, picks_ref, select, kept, dense):
    spans, _, side, _ = tiles_ref.shape
    owned = table_ref.shape[0]
    span_rows = ids_ref.shape[1] // spans
    rows_whole = dense.shape[0]
    chunk = min(256, owned)
    group = min(512, rows_whole)

    for span in range(spans):
        mine = slice(span * span_rows, (span + 1) * span_rows)

        def fill(i, _, span=span, mine=mine):
            first = pl.multiple_of(i * chunk, chunk)
            here = pl.ds(first, chunk)
            hot = chosen(ids_ref[:, mine], chunk, first)
            select[here, mine] = hot.astype(jnp.bfloat16)
            taken = jnp.max(hot, axis=1, keepdims=True)
            source = table_ref if span == 0 else kept
            kept[here, :] = jnp.where(taken > 0.5, 0.0, source[here, :].astype(jnp.float32)).astype(jnp.bfloat16)
            return 0

        lax.fori_loop(0, owned // chunk, fill, 0)
        dense[...] = jnp.zeros_like(dense)

        def place(t, _, span=span):
            row = pl.multiple_of(rows_ref[span, t] * side, side)
            col = pl.multiple_of(cols_ref[span, t] * side, side)
            dense[pl.ds(row, side), pl.ds(col, side)] = tiles_ref[span, t]
            return 0

        lax.fori_loop(0, counts_ref[span, 0], place, 0)
        width = (span + 1) * span_rows

        def multiply(i, _, span=span, width=width):
            here = pl.ds(pl.multiple_of(i * group, group), group)
            block = dense[here, :]
            base_ref[span, here, :] = jnp.dot(block, kept[...], preferred_element_type=jnp.float32)
            picks_ref[span, here, :width] = jnp.dot(
                block, select[:, :width], preferred_element_type=jnp.float32
            ).astype(jnp.bfloat16)
            if width < picks_ref.shape[2]:
                picks_ref[span, here, width:] = jnp.zeros((group, picks_ref.shape[2] - width), jnp.bfloat16)
            return 0

        lax.fori_loop(0, rows_whole // group, multiply, 0)


def relay(
    sections, vertices, feats,
    base_hbm, picks_hbm, initial_ref, weight_hbm, kept_hbm, select_hbm, out_ref, table_hbm,
    base_ref, picks_ref, weight_ref, kept_ref, select_ref, fresh_ref,
    arrived, partial, parts, passing, support, other, result,
    load_sem, table_sem, x_send, x_recv, p_send, p_recv, h_send, h_recv, s_send, s_recv,
):
    section = lax.axis_index("section")
    vertex = lax.axis_index("vertex")
    feat = lax.axis_index("feat")
    spans, span_rows, width = initial_ref.shape
    last = vertices - 1
    partner = lax.rem(feat + 1, feats)
    beta = jnp.log(BETA_SCALE / (section + 1).astype(jnp.float32) + 1.0)
    halves = 2
    piece = span_rows // halves
    relayed = vertices > 3

    loads = []
    for span in range(spans):
        loads.append(pltpu.make_async_copy(base_hbm.at[span], base_ref.at[span], load_sem.at[2 * span]))
        loads.append(pltpu.make_async_copy(picks_hbm.at[span], picks_ref.at[span], load_sem.at[2 * span + 1]))
    load_weight = pltpu.make_async_copy(weight_hbm, weight_ref, load_sem.at[2 * spans])
    load_kept = pltpu.make_async_copy(kept_hbm, kept_ref, load_sem.at[2 * spans + 1])
    load_select = pltpu.make_async_copy(select_hbm, select_ref, load_sem.at[2 * spans + 2])
    for load in [*loads[:2], load_weight, *loads[2:], load_kept, load_select]:
        load.start()

    barrier = pltpu.get_barrier_semaphore()
    for step in range(1, vertices):
        peer = lax.rem(vertex + step, vertices)
        pl.semaphore_signal(barrier, inc=1, device_id=(section, peer, feat), device_id_type=MESH)
    pl.semaphore_signal(barrier, inc=1, device_id=(section, vertex, partner), device_id_type=MESH)
    for step in (1, sections - 1):
        peer = lax.rem(section + step, sections)
        pl.semaphore_signal(barrier, inc=1, device_id=(peer, vertex, feat), device_id_type=MESH)
    if relayed:
        @pl.when(vertex == 0)
        def _():
            parts[:, 0] = jnp.zeros((spans, span_rows, width), jnp.bfloat16)

        @pl.when(vertex == last)
        def _():
            parts[:, last - 1] = jnp.zeros((spans, span_rows, width), jnp.bfloat16)

    pl.semaphore_wait(barrier, vertices - 1 + 1 + 2)

    def half_of(half):
        return slice(half * piece, (half + 1) * piece)

    def row_copy(span, half):
        rows = pl.ds(half * piece, piece)
        return pltpu.make_async_remote_copy(
            src_ref=result.at[span, rows], dst_ref=arrived.at[span, rows],
            send_sem=x_send.at[span, half], recv_sem=x_recv.at[span, half],
            device_id=(lax.rem(section + 1, sections), vertex, feat), device_id_type=MESH,
        )

    def chunk_rows(peer, half):
        return pl.ds(pl.multiple_of(peer * span_rows + half * piece, piece), piece)

    def part_copy(span, step, half):
        peer = lax.rem(vertex + step, vertices)
        return pltpu.make_async_remote_copy(
            src_ref=partial.at[span, chunk_rows(peer, half)],
            dst_ref=parts.at[span, step - 1, pl.ds(half * piece, piece)],
            send_sem=p_send.at[span, step - 1, half], recv_sem=p_recv.at[span, step - 1, half],
            device_id=(section, peer, feat), device_id_type=MESH,
        )

    def pass_copy(span, half):
        far = jnp.where(vertex == 0, last, 0)
        near = jnp.where(vertex == 0, 1, last - 1)
        return pltpu.make_async_remote_copy(
            src_ref=partial.at[span, chunk_rows(far, half)],
            dst_ref=passing.at[span, pl.ds(half * piece, piece)],
            send_sem=h_send.at[span, half], recv_sem=h_recv.at[span, half],
            device_id=(section, near, feat), device_id_type=MESH,
        )

    def support_copy(span, half):
        rows = pl.ds(half * piece, piece)
        return pltpu.make_async_remote_copy(
            src_ref=support.at[span, rows], dst_ref=other.at[span, rows],
            send_sem=s_send.at[span, half], recv_sem=s_recv.at[span, half],
            device_id=(section, vertex, partner), device_id_type=MESH,
        )

    at_end = (vertex == 0) | (vertex == last)

    def is_direct(step):
        if not relayed:
            return vertex >= 0
        peer = lax.rem(vertex + step, vertices)
        ends = ((vertex == 0) & (peer == last)) | ((vertex == last) & (peer == 0))
        inner = ((vertex == 1) & (peer == last)) | ((vertex == last - 1) & (peer == 0))
        return jnp.logical_not(ends | inner)

    def is_sent(step):
        if not relayed:
            return vertex >= 0
        peer = lax.rem(vertex + step, vertices)
        return jnp.logical_not(((vertex == 0) & (peer == last)) | ((vertex == last) & (peer == 0)))

    def is_received(step):
        if not relayed:
            return vertex >= 0
        source = lax.rem(vertex + vertices - step, vertices)
        return jnp.logical_not(((vertex == 0) & (source == last)) | ((vertex == last) & (source == 0)))

    def scatter(span):
        mine = slice(span * span_rows, (span + 1) * span_rows)
        loads[2 * span].wait()
        loads[2 * span + 1].wait()

        @pl.when(section == 0)
        def _():
            fresh_ref[mine, :] = initial_ref[span]

        @pl.when(section > 0)
        def _():
            for half in range(halves):
                row_copy(span, half).wait_recv()
            fresh_ref[mine, :] = arrived[span]

        used = (span + 1) * span_rows
        rows_now = fresh_ref[:used, :]

        def compute(peer):
            here = pl.ds(pl.multiple_of(peer * span_rows, span_rows), span_rows)
            total = base_ref[span, here, :] + jnp.dot(
                picks_ref[span, here, :used], rows_now, preferred_element_type=jnp.float32
            )
            partial[span, here, :] = total.astype(jnp.bfloat16)

        if relayed:
            @pl.when(at_end)
            def _():
                compute(jnp.where(vertex == 0, last, 0))
                for half in range(halves):
                    pass_copy(span, half).start()

        for step in range(1, vertices):
            @pl.when(is_sent(step))
            def _(step=step):
                compute(lax.rem(vertex + step, vertices))

            @pl.when(is_direct(step))
            def _(step=step):
                part_copy(span, step, 0).start()

        for half in range(1, halves):
            for step in range(1, vertices):
                @pl.when(is_direct(step))
                def _(step=step, half=half):
                    part_copy(span, step, half).start()

        compute(vertex)
        if relayed:
            for who, step in ((1, last - 1), (last - 1, 2)):
                @pl.when(vertex == who)
                def _(who=who, step=step):
                    far = last if who == 1 else 0
                    for half in range(halves):
                        pass_copy(span, half).wait_recv()
                        here = pl.ds(far * span_rows + half * piece, piece)
                        partial[span, here, :] = (
                            partial[span, here, :].astype(jnp.float32)
                            + passing[span, half_of(half), :].astype(jnp.float32)
                        ).astype(jnp.bfloat16)
                        part_copy(span, step, half).start()

    def finish(span, half):
        total = partial[span, chunk_rows(vertex, half), :].astype(jnp.float32)
        for step in range(1, vertices):
            @pl.when(is_received(step))
            def _(step=step):
                part_copy(span, step, half).wait_recv()

        for step in range(1, vertices):
            total += parts[span, step - 1, half_of(half), :].astype(jnp.float32)
        mixed = (
            (1.0 - RESIDUAL_SHARE) * total
            + RESIDUAL_SHARE * initial_ref[span, half_of(half), :].astype(jnp.float32)
        ).astype(jnp.bfloat16)
        support[span, half_of(half), :] = mixed
        support_copy(span, half).start()
        mine = pl.ds(pl.multiple_of(feat * width, width), width)
        theirs = pl.ds(pl.multiple_of(partner * width, width), width)
        projected = jnp.dot(mixed, weight_ref[mine, :], preferred_element_type=jnp.float32)
        support_copy(span, half).wait_recv()
        projected += jnp.dot(other[span, half_of(half), :], weight_ref[theirs, :], preferred_element_type=jnp.float32)
        rows = jnp.maximum((1.0 - beta) * mixed.astype(jnp.float32) + beta * projected, 0.0).astype(jnp.bfloat16)
        result[span, half_of(half), :] = rows
        out_ref[span, half_of(half), :] = rows

        @pl.when(section < sections - 1)
        def _():
            row_copy(span, half).start()

    scatter(0)
    load_weight.wait()
    for span in range(1, spans):
        scatter(span)
        for half in range(halves):
            finish(span - 1, half)

    load_kept.wait()
    load_select.wait()
    chunk = min(256, kept_ref.shape[0])

    def merge(i, _):
        here = pl.ds(pl.multiple_of(i * chunk, chunk), chunk)
        moved = jnp.dot(select_ref[here, :], fresh_ref[...], preferred_element_type=jnp.float32)
        kept_ref[here, :] = (kept_ref[here, :].astype(jnp.float32) + moved).astype(jnp.bfloat16)
        return 0

    lax.fori_loop(0, kept_ref.shape[0] // chunk, merge, 0)
    store = pltpu.make_async_copy(kept_ref, table_hbm, table_sem)
    store.start()
    for half in range(halves):
        finish(spans - 1, half)

    for span in range(spans):
        for half in range(halves):
            support_copy(span, half).wait_send()
            for step in range(1, vertices):
                @pl.when(is_sent(step))
                def _(span=span, step=step, half=half):
                    part_copy(span, step, half).wait_send()

            if relayed:
                @pl.when(at_end)
                def _(span=span, half=half):
                    pass_copy(span, half).wait_send()

            @pl.when(section < sections - 1)
            def _(span=span, half=half):
                row_copy(span, half).wait_send()

    store.wait()


def shards(sizes, features, history, weights, tile_values, tile_rows, tile_cols, tile_counts, span_ids):
    sections, vertices, feats = sizes
    spans, span_rows = span_ids.shape
    side = tile_values.shape[2]
    owned, width = features.shape
    rows_whole = span_rows * vertices
    table = history[0]
    ids_flat = span_ids.reshape(1, spans * span_rows)
    vmem = pl.BlockSpec(memory_space=pltpu.VMEM)
    smem = pl.BlockSpec(memory_space=pltpu.SMEM)
    initial = jnp.take(features, span_ids.reshape(-1), axis=0, mode="clip").reshape(spans, span_rows, width)

    rows_all = spans * span_rows
    base, picks, select, kept = pl.pallas_call(
        prepare,
        name="prepare",
        out_shape=(
            jax.ShapeDtypeStruct((spans, rows_whole, width), jnp.float32),
            jax.ShapeDtypeStruct((spans, rows_whole, rows_all), jnp.bfloat16),
            jax.ShapeDtypeStruct((owned, rows_all), jnp.bfloat16),
            jax.ShapeDtypeStruct((owned, width), jnp.bfloat16),
        ),
        in_specs=[smem, smem, smem, vmem, vmem, vmem],
        out_specs=(vmem,) * 4,
        scratch_shapes=[pltpu.VMEM((rows_whole, owned), jnp.bfloat16)],
        compiler_params=pltpu.CompilerParams(vmem_limit_bytes=VMEM_BYTES),
    )(tile_rows, tile_cols, tile_counts, ids_flat, tile_values, table)

    anywhere = pl.BlockSpec(memory_space=pl.ANY)
    block = pltpu.VMEM((spans, span_rows, width), jnp.bfloat16)
    halves = 2
    layer_rows, table_new = pl.pallas_call(
        functools.partial(relay, sections, vertices, feats),
        name="relay",
        out_shape=(
            jax.ShapeDtypeStruct((spans, span_rows, width), jnp.bfloat16),
            jax.ShapeDtypeStruct((owned, width), jnp.bfloat16),
        ),
        in_specs=[anywhere, anywhere, vmem, anywhere, anywhere, anywhere],
        out_specs=(vmem, anywhere),
        scratch_shapes=[
            pltpu.VMEM(base.shape, base.dtype),
            pltpu.VMEM(picks.shape, picks.dtype),
            pltpu.VMEM(weights.shape[1:], weights.dtype),
            pltpu.VMEM(kept.shape, kept.dtype),
            pltpu.VMEM(select.shape, select.dtype),
            pltpu.VMEM((rows_all, width), jnp.bfloat16),
            block,
            pltpu.VMEM((spans, rows_whole, width), jnp.bfloat16),
            pltpu.VMEM((spans, vertices - 1, span_rows, width), jnp.bfloat16),
            block, block, block, block,
            pltpu.SemaphoreType.DMA((2 * spans + 3,)),
            pltpu.SemaphoreType.DMA,
            pltpu.SemaphoreType.DMA((spans, halves)),
            pltpu.SemaphoreType.DMA((spans, halves)),
            pltpu.SemaphoreType.DMA((spans, vertices - 1, halves)),
            pltpu.SemaphoreType.DMA((spans, vertices - 1, halves)),
            pltpu.SemaphoreType.DMA((spans, halves)),
            pltpu.SemaphoreType.DMA((spans, halves)),
            pltpu.SemaphoreType.DMA((spans, halves)),
            pltpu.SemaphoreType.DMA((spans, halves)),
        ],
        compiler_params=pltpu.CompilerParams(
            vmem_limit_bytes=VMEM_BYTES, collective_id=0, has_side_effects=True
        ),
    )(base, picks, initial, weights[0], kept, select)
    return (layer_rows[None], table_new[None])


def solution(mesh):
    placed = (
        P("vertex", "feat"),
        P("section", "vertex", "feat"),
        P("section", None, "feat"),
        P(None, "vertex", None, None),
        P(None, "vertex"),
        P(None, "vertex"),
        P(None, "vertex"),
        P(None, "vertex"),
    )
    sizes = (mesh.shape["section"], mesh.shape["vertex"], mesh.shape["feat"])
    return jax.shard_map(
        functools.partial(shards, sizes),
        mesh=mesh,
        in_specs=placed,
        out_specs=(P("section", None, "vertex", "feat"), P("section", "vertex", "feat")),
        check_vma=False,
    )
```

```python
import functools

import jax
import jax.numpy as jnp
from jax import lax
from jax.experimental import pallas as pl
from jax.experimental.pallas import tpu as pltpu
from jax.sharding import PartitionSpec as P

RESIDUAL_SHARE = 0.2
BETA_SCALE = 0.5
MESH = pl.DeviceIdType.MESH
VMEM_BYTES = 60_000 * 1024


def chosen(ids_row, rows, first=0):
    shape = (rows, ids_row.shape[1])
    return (lax.broadcasted_iota(jnp.int32, shape, 0) + first == ids_row).astype(jnp.float32)


def prepare(
    rows_ref, cols_ref, counts_ref, ids_ref, tiles_ref, features_ref, dense_hbm, select_hbm, initial_ref,
    dense, select, dense_sem, select_sem,
):
    spans, _, side, _ = tiles_ref.shape
    span_rows = ids_ref.shape[1]
    owned = select.shape[0]
    copies = []
    for span in range(spans):
        dense[span] = jnp.zeros(dense.shape[1:], dense.dtype)

        def place(t, _, span=span):
            row = pl.multiple_of(rows_ref[span, t] * side, side)
            col = pl.multiple_of(cols_ref[span, t] * side, side)
            dense[span, pl.ds(row, side), pl.ds(col, side)] = tiles_ref[span, t]
            return 0

        lax.fori_loop(0, counts_ref[0, span], place, 0)
        copies.append(pltpu.make_async_copy(dense.at[span], dense_hbm.at[span], dense_sem.at[span]))
        copies[-1].start()

    for span in range(spans):
        mine = slice(span * span_rows, (span + 1) * span_rows)
        select[:, mine] = chosen(ids_ref[span : span + 1, :], owned).astype(jnp.bfloat16)
    copies.append(pltpu.make_async_copy(select, select_hbm, select_sem))
    copies[-1].start()
    initial_ref[...] = lax.dot_general(
        select[...], features_ref[...], (((0,), (0,)), ((), ())), preferred_element_type=jnp.float32
    ).astype(jnp.bfloat16)
    for copy in copies:
        copy.wait()


def relay(
    sections, vertices, feats,
    dense_hbm, initial_ref, weight_hbm, kept_hbm, select_hbm, out_ref, table_hbm,
    dense, base_ref, picks_ref, weight_ref, kept_ref, select_ref, fresh_ref,
    arrived, partial, parts, passing, support, other, result,
    load_sem, table_sem, x_send, x_recv, p_send, p_recv, h_send, h_recv, s_send, s_recv,
):
    section = lax.axis_index("section")
    vertex = lax.axis_index("vertex")
    feat = lax.axis_index("feat")
    spans, span_rows, width = initial_ref.shape
    last = vertices - 1
    partner = lax.rem(feat + 1, feats)
    beta = jnp.log(BETA_SCALE / (section + 1).astype(jnp.float32) + 1.0)
    halves = 2
    piece = span_rows // halves
    relayed = vertices > 3

    rows_whole = dense.shape[1]
    owned = kept_ref.shape[0]
    group = min(512, rows_whole)
    chunk = min(256, owned)

    def load_dense(span):
        return pltpu.make_async_copy(dense_hbm.at[span], dense.at[span % 2], load_sem.at[span])

    load_weight = pltpu.make_async_copy(weight_hbm, weight_ref, load_sem.at[spans])
    load_kept = pltpu.make_async_copy(kept_hbm, kept_ref, load_sem.at[spans + 1])
    load_select = pltpu.make_async_copy(select_hbm, select_ref, load_sem.at[spans + 2])
    load_kept.start()
    load_select.start()
    for span in range(min(2, spans)):
        load_dense(span).start()
    load_weight.start()

    barrier = pltpu.get_barrier_semaphore()
    for step in range(1, vertices):
        peer = lax.rem(vertex + step, vertices)
        pl.semaphore_signal(barrier, inc=1, device_id=(section, peer, feat), device_id_type=MESH)
    pl.semaphore_signal(barrier, inc=1, device_id=(section, vertex, partner), device_id_type=MESH)
    for step in (1, sections - 1):
        peer = lax.rem(section + step, sections)
        pl.semaphore_signal(barrier, inc=1, device_id=(peer, vertex, feat), device_id_type=MESH)
    if relayed:
        @pl.when(vertex == 0)
        def _():
            parts[:, 0] = jnp.zeros((spans, span_rows, width), jnp.bfloat16)

        @pl.when(vertex == last)
        def _():
            parts[:, last - 1] = jnp.zeros((spans, span_rows, width), jnp.bfloat16)

    pl.semaphore_wait(barrier, vertices - 1 + 1 + 2)

    def half_of(half):
        return slice(half * piece, (half + 1) * piece)

    def row_copy(span, half):
        rows = pl.ds(half * piece, piece)
        return pltpu.make_async_remote_copy(
            src_ref=result.at[span, rows], dst_ref=arrived.at[span, rows],
            send_sem=x_send.at[span, half], recv_sem=x_recv.at[span, half],
            device_id=(lax.rem(section + 1, sections), vertex, feat), device_id_type=MESH,
        )

    def chunk_rows(peer, half):
        return pl.ds(pl.multiple_of(peer * span_rows + half * piece, piece), piece)

    def part_copy(span, step, half):
        peer = lax.rem(vertex + step, vertices)
        return pltpu.make_async_remote_copy(
            src_ref=partial.at[span, chunk_rows(peer, half)],
            dst_ref=parts.at[span, step - 1, pl.ds(half * piece, piece)],
            send_sem=p_send.at[span, step - 1, half], recv_sem=p_recv.at[span, step - 1, half],
            device_id=(section, peer, feat), device_id_type=MESH,
        )

    def pass_copy(span, half):
        far = jnp.where(vertex == 0, last, 0)
        near = jnp.where(vertex == 0, 1, last - 1)
        return pltpu.make_async_remote_copy(
            src_ref=partial.at[span, chunk_rows(far, half)],
            dst_ref=passing.at[span, pl.ds(half * piece, piece)],
            send_sem=h_send.at[span, half], recv_sem=h_recv.at[span, half],
            device_id=(section, near, feat), device_id_type=MESH,
        )

    def support_copy(span, half):
        rows = pl.ds(half * piece, piece)
        return pltpu.make_async_remote_copy(
            src_ref=support.at[span, rows], dst_ref=other.at[span, rows],
            send_sem=s_send.at[span, half], recv_sem=s_recv.at[span, half],
            device_id=(section, vertex, partner), device_id_type=MESH,
        )

    at_end = (vertex == 0) | (vertex == last)

    def is_direct(step):
        if not relayed:
            return vertex >= 0
        peer = lax.rem(vertex + step, vertices)
        ends = ((vertex == 0) & (peer == last)) | ((vertex == last) & (peer == 0))
        inner = ((vertex == 1) & (peer == last)) | ((vertex == last - 1) & (peer == 0))
        return jnp.logical_not(ends | inner)

    def is_sent(step):
        if not relayed:
            return vertex >= 0
        peer = lax.rem(vertex + step, vertices)
        return jnp.logical_not(((vertex == 0) & (peer == last)) | ((vertex == last) & (peer == 0)))

    def is_received(step):
        if not relayed:
            return vertex >= 0
        source = lax.rem(vertex + vertices - step, vertices)
        return jnp.logical_not(((vertex == 0) & (source == last)) | ((vertex == last) & (source == 0)))

    def local(span):
        mine = slice(span * span_rows, (span + 1) * span_rows)
        used = (span + 1) * span_rows
        if span == 0:
            load_kept.wait()
            load_select.wait()

        def clear(i, _):
            here = pl.ds(pl.multiple_of(i * chunk, chunk), chunk)
            taken = jnp.max(select_ref[here, mine].astype(jnp.float32), axis=1, keepdims=True)
            kept_ref[here, :] = jnp.where(taken > 0.5, 0.0, kept_ref[here, :].astype(jnp.float32)).astype(jnp.bfloat16)
            return 0

        lax.fori_loop(0, owned // chunk, clear, 0)
        load_dense(span).wait()

        def multiply(i, _):
            here = pl.ds(pl.multiple_of(i * group, group), group)
            block = dense[span % 2, here, :]
            base_ref[span, here, :] = jnp.dot(block, kept_ref[...], preferred_element_type=jnp.float32)
            picks_ref[span, here, :used] = jnp.dot(
                block, select_ref[:, :used], preferred_element_type=jnp.float32
            ).astype(jnp.bfloat16)
            return 0

        lax.fori_loop(0, rows_whole // group, multiply, 0)
        if span + 2 < spans:
            load_dense(span + 2).start()

    def scatter(span):
        mine = slice(span * span_rows, (span + 1) * span_rows)
        @pl.when(section == 0)
        def _():
            fresh_ref[mine, :] = initial_ref[span]

        @pl.when(section > 0)
        def _():
            for half in range(halves):
                row_copy(span, half).wait_recv()
            fresh_ref[mine, :] = arrived[span]

        used = (span + 1) * span_rows
        rows_now = fresh_ref[:used, :]

        def compute(peer):
            here = pl.ds(pl.multiple_of(peer * span_rows, span_rows), span_rows)
            total = base_ref[span, here, :] + jnp.dot(
                picks_ref[span, here, :used], rows_now, preferred_element_type=jnp.float32
            )
            partial[span, here, :] = total.astype(jnp.bfloat16)

        if relayed:
            @pl.when(at_end)
            def _():
                compute(jnp.where(vertex == 0, last, 0))
                for half in range(halves):
                    pass_copy(span, half).start()

        for step in range(1, vertices):
            @pl.when(is_sent(step))
            def _(step=step):
                compute(lax.rem(vertex + step, vertices))

            @pl.when(is_direct(step))
            def _(step=step):
                part_copy(span, step, 0).start()

        for half in range(1, halves):
            for step in range(1, vertices):
                @pl.when(is_direct(step))
                def _(step=step, half=half):
                    part_copy(span, step, half).start()

        compute(vertex)
        if relayed:
            for who, step in ((1, last - 1), (last - 1, 2)):
                @pl.when(vertex == who)
                def _(who=who, step=step):
                    far = last if who == 1 else 0
                    for half in range(halves):
                        pass_copy(span, half).wait_recv()
                        here = pl.ds(far * span_rows + half * piece, piece)
                        partial[span, here, :] = (
                            partial[span, here, :].astype(jnp.float32)
                            + passing[span, half_of(half), :].astype(jnp.float32)
                        ).astype(jnp.bfloat16)
                        part_copy(span, step, half).start()

    def finish(span, half):
        total = partial[span, chunk_rows(vertex, half), :].astype(jnp.float32)
        for step in range(1, vertices):
            @pl.when(is_received(step))
            def _(step=step):
                part_copy(span, step, half).wait_recv()

        for step in range(1, vertices):
            total += parts[span, step - 1, half_of(half), :].astype(jnp.float32)
        mixed = (
            (1.0 - RESIDUAL_SHARE) * total
            + RESIDUAL_SHARE * initial_ref[span, half_of(half), :].astype(jnp.float32)
        ).astype(jnp.bfloat16)
        support[span, half_of(half), :] = mixed
        support_copy(span, half).start()
        mine = pl.ds(pl.multiple_of(feat * width, width), width)
        theirs = pl.ds(pl.multiple_of(partner * width, width), width)
        projected = jnp.dot(mixed, weight_ref[mine, :], preferred_element_type=jnp.float32)
        support_copy(span, half).wait_recv()
        projected += jnp.dot(other[span, half_of(half), :], weight_ref[theirs, :], preferred_element_type=jnp.float32)
        rows = jnp.maximum((1.0 - beta) * mixed.astype(jnp.float32) + beta * projected, 0.0).astype(jnp.bfloat16)
        result[span, half_of(half), :] = rows
        out_ref[span, half_of(half), :] = rows

        @pl.when(section < sections - 1)
        def _():
            row_copy(span, half).start()

    @pl.when(section > 0)
    def _():
        for span in range(spans):
            local(span)

    for span in range(spans):
        @pl.when(section == 0)
        def _(span=span):
            local(span)

        scatter(span)
        if span == 0:
            load_weight.wait()
        for half in range(halves if span else 0):
            finish(span - 1, half)

    def merge(i, _):
        here = pl.ds(pl.multiple_of(i * chunk, chunk), chunk)
        moved = jnp.dot(select_ref[here, :], fresh_ref[...], preferred_element_type=jnp.float32)
        kept_ref[here, :] = (kept_ref[here, :].astype(jnp.float32) + moved).astype(jnp.bfloat16)
        return 0

    lax.fori_loop(0, owned // chunk, merge, 0)
    store = pltpu.make_async_copy(kept_ref, table_hbm, table_sem)
    store.start()
    for half in range(halves):
        finish(spans - 1, half)

    for span in range(spans):
        for half in range(halves):
            support_copy(span, half).wait_send()
            for step in range(1, vertices):
                @pl.when(is_sent(step))
                def _(span=span, step=step, half=half):
                    part_copy(span, step, half).wait_send()

            if relayed:
                @pl.when(at_end)
                def _(span=span, half=half):
                    pass_copy(span, half).wait_send()

            @pl.when(section < sections - 1)
            def _(span=span, half=half):
                row_copy(span, half).wait_send()

    store.wait()


def deliver(rows_hbm, table_hbm, rows_out, table_out, rows_ref, table_ref, in_sem, out_sem):
    chunks = in_sem.shape[0] - 1
    size = table_ref.shape[0] // chunks
    moves = []
    for i in range(chunks):
        here = pl.ds(i * size, size)
        moves.append((
            pltpu.make_async_copy(table_hbm.at[here], table_ref.at[here], in_sem.at[i]),
            pltpu.make_async_copy(table_ref.at[here], table_out.at[here], out_sem.at[i]),
        ))
    moves.append((
        pltpu.make_async_copy(rows_hbm, rows_ref, in_sem.at[chunks]),
        pltpu.make_async_copy(rows_ref, rows_out, out_sem.at[chunks]),
    ))
    for get, _ in moves:
        get.start()
    for get, put in moves:
        get.wait()
        put.start()
    for _, put in moves:
        put.wait()


def shards(sizes, features, history, weights, tile_values, tile_rows, tile_cols, tile_counts, span_ids):
    sections, vertices, feats = sizes
    spans, span_rows = span_ids.shape
    side = tile_values.shape[2]
    owned, width = features.shape
    rows_whole = span_rows * vertices
    rows_all = spans * span_rows
    vmem = pl.BlockSpec(memory_space=pltpu.VMEM)
    smem = pl.BlockSpec(memory_space=pltpu.SMEM)
    anywhere = pl.BlockSpec(memory_space=pl.ANY)

    dense, select, initial = pl.pallas_call(
        prepare,
        name="prepare",
        out_shape=(
            jax.ShapeDtypeStruct((spans, rows_whole, owned), jnp.bfloat16),
            jax.ShapeDtypeStruct((owned, rows_all), jnp.bfloat16),
            jax.ShapeDtypeStruct((rows_all, width), jnp.bfloat16),
        ),
        in_specs=[smem, smem, smem, vmem, vmem, vmem],
        out_specs=(anywhere, anywhere, vmem),
        scratch_shapes=[
            pltpu.VMEM((spans, rows_whole, owned), jnp.bfloat16),
            pltpu.VMEM((owned, rows_all), jnp.bfloat16),
            pltpu.SemaphoreType.DMA((spans,)),
            pltpu.SemaphoreType.DMA,
        ],
        compiler_params=pltpu.CompilerParams(vmem_limit_bytes=VMEM_BYTES),
    )(tile_rows, tile_cols, tile_counts.reshape(1, spans), span_ids, tile_values, features)

    rows_type = jax.ShapeDtypeStruct((spans, span_rows, width), jnp.bfloat16)
    table_type = jax.ShapeDtypeStruct((owned, width), jnp.bfloat16)
    block = pltpu.VMEM(rows_type.shape, jnp.bfloat16)
    halves = 2
    pair = pltpu.SemaphoreType.DMA((spans, halves))
    layer_rows, table_new = pl.pallas_call(
        functools.partial(relay, sections, vertices, feats),
        name="relay",
        out_shape=(rows_type, table_type),
        in_specs=[anywhere, vmem, anywhere, anywhere, anywhere],
        out_specs=(vmem, anywhere),
        scratch_shapes=[
            pltpu.VMEM((min(2, spans), rows_whole, owned), jnp.bfloat16),
            pltpu.VMEM((spans, rows_whole, width), jnp.float32),
            pltpu.VMEM((spans, rows_whole, rows_all), jnp.bfloat16),
            pltpu.VMEM(weights.shape[1:], weights.dtype),
            pltpu.VMEM((owned, width), jnp.bfloat16),
            pltpu.VMEM(select.shape, select.dtype),
            pltpu.VMEM((rows_all, width), jnp.bfloat16),
            block,
            pltpu.VMEM((spans, rows_whole, width), jnp.bfloat16),
            pltpu.VMEM((spans, vertices - 1, span_rows, width), jnp.bfloat16),
            block, block, block, block,
            pltpu.SemaphoreType.DMA((spans + 3,)),
            pltpu.SemaphoreType.DMA,
            pair, pair,
            pltpu.SemaphoreType.DMA((spans, vertices - 1, halves)),
            pltpu.SemaphoreType.DMA((spans, vertices - 1, halves)),
            pair, pair, pair, pair,
        ],
        compiler_params=pltpu.CompilerParams(
            vmem_limit_bytes=VMEM_BYTES, collective_id=0, has_side_effects=True
        ),
    )(dense, initial.reshape(rows_type.shape), weights[0], history[0], select)

    chunks = 8
    layer_rows, table_new = pl.pallas_call(
        deliver,
        name="deliver",
        out_shape=(rows_type, table_type),
        in_specs=[anywhere, anywhere],
        out_specs=(anywhere, anywhere),
        scratch_shapes=[
            block,
            pltpu.VMEM(table_type.shape, jnp.bfloat16),
            pltpu.SemaphoreType.DMA((chunks + 1,)),
            pltpu.SemaphoreType.DMA((chunks + 1,)),
        ],
        compiler_params=pltpu.CompilerParams(vmem_limit_bytes=VMEM_BYTES),
    )(layer_rows, table_new)
    return (layer_rows[None], table_new[None])


def solution(mesh):
    placed = (
        P("vertex", "feat"),
        P("section", "vertex", "feat"),
        P("section", None, "feat"),
        P(None, "vertex", None, None),
        P(None, "vertex"),
        P(None, "vertex"),
        P(None, "vertex"),
        P(None, "vertex"),
    )
    sizes = (mesh.shape["section"], mesh.shape["vertex"], mesh.shape["feat"])
    return jax.shard_map(
        functools.partial(shards, sizes),
        mesh=mesh,
        in_specs=placed,
        out_specs=(P("section", None, "vertex", "feat"), P("section", "vertex", "feat")),
        check_vma=False,
    )
```

```python
import functools

import jax
import jax.numpy as jnp
from jax import lax
from jax.experimental import pallas as pl
from jax.experimental.pallas import tpu as pltpu
from jax.sharding import PartitionSpec as P

RESIDUAL_SHARE = 0.2
BETA_SCALE = 0.5
MESH = pl.DeviceIdType.MESH
VMEM_BYTES = 60_000 * 1024


def chosen(ids_row, rows, first=0):
    shape = (rows, ids_row.shape[1])
    return (lax.broadcasted_iota(jnp.int32, shape, 0) + first == ids_row).astype(jnp.float32)


def prepare(rows_ref, cols_ref, counts_ref, tiles_ref, dense_hbm, dense, dense_sem):
    spans, _, side, _ = tiles_ref.shape
    copies = []
    for span in range(spans):
        dense[span] = jnp.zeros(dense.shape[1:], dense.dtype)

        def place(t, _, span=span):
            row = pl.multiple_of(rows_ref[span, t] * side, side)
            col = pl.multiple_of(cols_ref[span, t] * side, side)
            dense[span, pl.ds(row, side), pl.ds(col, side)] = tiles_ref[span, t]
            return 0

        lax.fori_loop(0, counts_ref[0, span], place, 0)
        copies.append(pltpu.make_async_copy(dense.at[span], dense_hbm.at[span], dense_sem.at[span]))
        copies[-1].start()
    for copy in copies:
        copy.wait()


def relay(
    sections, vertices, feats,
    dense_hbm, ids_ref, weight_hbm, kept_hbm, features_hbm, out_ref, table_hbm,
    dense, base_ref, picks_ref, weight_ref, kept_ref, features_ref, select_ref, initial_ref, fresh_ref,
    arrived, partial, parts, passing, support, other, result,
    load_sem, table_sem, x_send, x_recv, p_send, p_recv, h_send, h_recv, s_send, s_recv,
):
    section = lax.axis_index("section")
    vertex = lax.axis_index("vertex")
    feat = lax.axis_index("feat")
    spans, span_rows, width = arrived.shape
    last = vertices - 1
    partner = lax.rem(feat + 1, feats)
    beta = jnp.log(BETA_SCALE / (section + 1).astype(jnp.float32) + 1.0)
    halves = 2
    piece = span_rows // halves
    relayed = vertices > 3

    rows_whole = dense.shape[1]
    owned = kept_ref.shape[0]
    group = min(512, rows_whole)
    chunk = min(256, owned)

    def load_dense(span):
        return pltpu.make_async_copy(dense_hbm.at[span], dense.at[span % 2], load_sem.at[span])

    load_weight = pltpu.make_async_copy(weight_hbm, weight_ref, load_sem.at[spans])
    load_kept = pltpu.make_async_copy(kept_hbm, kept_ref, load_sem.at[spans + 1])
    load_features = pltpu.make_async_copy(features_hbm, features_ref, load_sem.at[spans + 2])
    load_kept.start()
    load_features.start()
    for span in range(min(2, spans)):
        load_dense(span).start()
    load_weight.start()

    barrier = pltpu.get_barrier_semaphore()
    for step in range(1, vertices):
        peer = lax.rem(vertex + step, vertices)
        pl.semaphore_signal(barrier, inc=1, device_id=(section, peer, feat), device_id_type=MESH)
    pl.semaphore_signal(barrier, inc=1, device_id=(section, vertex, partner), device_id_type=MESH)
    for step in (1, sections - 1):
        peer = lax.rem(section + step, sections)
        pl.semaphore_signal(barrier, inc=1, device_id=(peer, vertex, feat), device_id_type=MESH)
    if relayed:
        @pl.when(vertex == 0)
        def _():
            parts[:, 0] = jnp.zeros((spans, span_rows, width), jnp.bfloat16)

        @pl.when(vertex == last)
        def _():
            parts[:, last - 1] = jnp.zeros((spans, span_rows, width), jnp.bfloat16)

    pl.semaphore_wait(barrier, vertices - 1 + 1 + 2)

    def half_of(half):
        return slice(half * piece, (half + 1) * piece)

    def row_copy(span, half):
        rows = pl.ds(half * piece, piece)
        return pltpu.make_async_remote_copy(
            src_ref=result.at[span, rows], dst_ref=arrived.at[span, rows],
            send_sem=x_send.at[span, half], recv_sem=x_recv.at[span, half],
            device_id=(lax.rem(section + 1, sections), vertex, feat), device_id_type=MESH,
        )

    def chunk_rows(peer, half):
        return pl.ds(pl.multiple_of(peer * span_rows + half * piece, piece), piece)

    def part_copy(span, step, half):
        peer = lax.rem(vertex + step, vertices)
        return pltpu.make_async_remote_copy(
            src_ref=partial.at[span, chunk_rows(peer, half)],
            dst_ref=parts.at[span, step - 1, pl.ds(half * piece, piece)],
            send_sem=p_send.at[span, step - 1, half], recv_sem=p_recv.at[span, step - 1, half],
            device_id=(section, peer, feat), device_id_type=MESH,
        )

    def pass_copy(span, half):
        far = jnp.where(vertex == 0, last, 0)
        near = jnp.where(vertex == 0, 1, last - 1)
        return pltpu.make_async_remote_copy(
            src_ref=partial.at[span, chunk_rows(far, half)],
            dst_ref=passing.at[span, pl.ds(half * piece, piece)],
            send_sem=h_send.at[span, half], recv_sem=h_recv.at[span, half],
            device_id=(section, near, feat), device_id_type=MESH,
        )

    def support_copy(span, half):
        rows = pl.ds(half * piece, piece)
        return pltpu.make_async_remote_copy(
            src_ref=support.at[span, rows], dst_ref=other.at[span, rows],
            send_sem=s_send.at[span, half], recv_sem=s_recv.at[span, half],
            device_id=(section, vertex, partner), device_id_type=MESH,
        )

    at_end = (vertex == 0) | (vertex == last)

    def is_direct(step):
        if not relayed:
            return vertex >= 0
        peer = lax.rem(vertex + step, vertices)
        ends = ((vertex == 0) & (peer == last)) | ((vertex == last) & (peer == 0))
        inner = ((vertex == 1) & (peer == last)) | ((vertex == last - 1) & (peer == 0))
        return jnp.logical_not(ends | inner)

    def is_sent(step):
        if not relayed:
            return vertex >= 0
        peer = lax.rem(vertex + step, vertices)
        return jnp.logical_not(((vertex == 0) & (peer == last)) | ((vertex == last) & (peer == 0)))

    def is_received(step):
        if not relayed:
            return vertex >= 0
        source = lax.rem(vertex + vertices - step, vertices)
        return jnp.logical_not(((vertex == 0) & (source == last)) | ((vertex == last) & (source == 0)))

    def local(span, leading):
        mine = slice(span * span_rows, (span + 1) * span_rows)
        used = (span + 1) * span_rows

        def clear(i, _):
            first = pl.multiple_of(i * chunk, chunk)
            here = pl.ds(first, chunk)
            hot = chosen(ids_ref[span : span + 1, :], chunk, first)
            select_ref[here, mine] = hot.astype(jnp.bfloat16)
            taken = jnp.max(hot, axis=1, keepdims=True) > 0.5
            filler = features_ref[here, :].astype(jnp.float32) if leading else 0.0
            kept_ref[here, :] = jnp.where(taken, filler, kept_ref[here, :].astype(jnp.float32)).astype(jnp.bfloat16)
            return 0

        lax.fori_loop(0, owned // chunk, clear, 0)
        load_dense(span).wait()

        def multiply(i, _):
            here = pl.ds(pl.multiple_of(i * group, group), group)
            block = dense[span % 2, here, :]
            product = jnp.dot(block, kept_ref[...], preferred_element_type=jnp.float32)
            if leading:
                partial[span, here, :] = product.astype(jnp.bfloat16)
            else:
                base_ref[span, here, :] = product
                picks_ref[span, here, :used] = jnp.dot(
                    block, select_ref[:, :used], preferred_element_type=jnp.float32
                ).astype(jnp.bfloat16)
            return 0

        lax.fori_loop(0, rows_whole // group, multiply, 0)
        if span + 2 < spans:
            load_dense(span + 2).start()

    def gather():
        initial_ref[...] = lax.dot_general(
            select_ref[...], features_ref[...], (((0,), (0,)), ((), ())), preferred_element_type=jnp.float32
        ).astype(jnp.bfloat16)

    def scatter(span):
        mine = slice(span * span_rows, (span + 1) * span_rows)
        @pl.when(section > 0)
        def _():
            for half in range(halves):
                row_copy(span, half).wait_recv()
            fresh_ref[mine, :] = arrived[span]

        used = (span + 1) * span_rows

        def compute(peer):
            here = pl.ds(pl.multiple_of(peer * span_rows, span_rows), span_rows)
            total = base_ref[span, here, :] + jnp.dot(
                picks_ref[span, here, :used], fresh_ref[:used, :], preferred_element_type=jnp.float32
            )
            partial[span, here, :] = total.astype(jnp.bfloat16)

        if relayed:
            @pl.when(at_end & (section > 0))
            def _():
                compute(jnp.where(vertex == 0, last, 0))

            @pl.when(at_end)
            def _():
                for half in range(halves):
                    pass_copy(span, half).start()

        for step in range(1, vertices):
            @pl.when(is_sent(step) & (section > 0))
            def _(step=step):
                compute(lax.rem(vertex + step, vertices))

            @pl.when(is_direct(step))
            def _(step=step):
                part_copy(span, step, 0).start()

        for half in range(1, halves):
            for step in range(1, vertices):
                @pl.when(is_direct(step))
                def _(step=step, half=half):
                    part_copy(span, step, half).start()

        @pl.when(section > 0)
        def _():
            compute(vertex)

    def pass_on(span):
        if relayed:
            for who, step in ((1, last - 1), (last - 1, 2)):
                @pl.when(vertex == who)
                def _(who=who, step=step):
                    far = last if who == 1 else 0
                    for half in range(halves):
                        pass_copy(span, half).wait_recv()
                        here = pl.ds(far * span_rows + half * piece, piece)
                        partial[span, here, :] = (
                            partial[span, here, :].astype(jnp.float32)
                            + passing[span, half_of(half), :].astype(jnp.float32)
                        ).astype(jnp.bfloat16)
                        part_copy(span, step, half).start()

    def finish(span, half):
        total = partial[span, chunk_rows(vertex, half), :].astype(jnp.float32)
        for step in range(1, vertices):
            @pl.when(is_received(step))
            def _(step=step):
                part_copy(span, step, half).wait_recv()

        for step in range(1, vertices):
            total += parts[span, step - 1, half_of(half), :].astype(jnp.float32)
        mixed = (
            (1.0 - RESIDUAL_SHARE) * total
            + RESIDUAL_SHARE * initial_ref[pl.ds(span * span_rows + half * piece, piece), :].astype(jnp.float32)
        ).astype(jnp.bfloat16)
        support[span, half_of(half), :] = mixed
        support_copy(span, half).start()
        mine = pl.ds(pl.multiple_of(feat * width, width), width)
        theirs = pl.ds(pl.multiple_of(partner * width, width), width)
        projected = jnp.dot(mixed, weight_ref[mine, :], preferred_element_type=jnp.float32)
        support_copy(span, half).wait_recv()
        projected += jnp.dot(other[span, half_of(half), :], weight_ref[theirs, :], preferred_element_type=jnp.float32)
        rows = jnp.maximum((1.0 - beta) * mixed.astype(jnp.float32) + beta * projected, 0.0).astype(jnp.bfloat16)
        result[span, half_of(half), :] = rows
        out_ref[span, half_of(half), :] = rows

        @pl.when(section < sections - 1)
        def _():
            row_copy(span, half).start()

    def finish_all(span):
        for half in range(halves):
            finish(span, half)

    load_kept.wait()
    load_features.wait()

    @pl.when(section == 0)
    def _():
        for span in range(spans):
            local(span, True)
            scatter(span)
            if span:
                pass_on(span - 1)
        gather()
        load_weight.wait()
        for span in range(spans - 1):
            finish_all(span)
            if span == 0:
                pass_on(spans - 1)

    @pl.when(section > 0)
    def _():
        for span in range(spans):
            local(span, False)
        gather()
        load_weight.wait()
        for span in range(spans):
            scatter(span)
            pass_on(span)
            if span:
                finish_all(span - 1)

    def merge(i, _):
        here = pl.ds(pl.multiple_of(i * chunk, chunk), chunk)
        moved = jnp.dot(select_ref[here, :], fresh_ref[...], preferred_element_type=jnp.float32)
        kept_ref[here, :] = (kept_ref[here, :].astype(jnp.float32) + moved).astype(jnp.bfloat16)
        return 0

    @pl.when(section > 0)
    def _():
        lax.fori_loop(0, owned // chunk, merge, 0)

    store = pltpu.make_async_copy(kept_ref, table_hbm, table_sem)
    store.start()
    finish_all(spans - 1)

    for span in range(spans):
        for half in range(halves):
            support_copy(span, half).wait_send()
            for step in range(1, vertices):
                @pl.when(is_sent(step))
                def _(span=span, step=step, half=half):
                    part_copy(span, step, half).wait_send()

            if relayed:
                @pl.when(at_end)
                def _(span=span, half=half):
                    pass_copy(span, half).wait_send()

            @pl.when(section < sections - 1)
            def _(span=span, half=half):
                row_copy(span, half).wait_send()

    store.wait()


def deliver(rows_hbm, table_hbm, rows_out, table_out, rows_ref, table_ref, in_sem, out_sem):
    chunks = in_sem.shape[0] - 1
    size = table_ref.shape[0] // chunks
    moves = []
    for i in range(chunks):
        here = pl.ds(i * size, size)
        moves.append((
            pltpu.make_async_copy(table_hbm.at[here], table_ref.at[here], in_sem.at[i]),
            pltpu.make_async_copy(table_ref.at[here], table_out.at[here], out_sem.at[i]),
        ))
    moves.append((
        pltpu.make_async_copy(rows_hbm, rows_ref, in_sem.at[chunks]),
        pltpu.make_async_copy(rows_ref, rows_out, out_sem.at[chunks]),
    ))
    for get, _ in moves:
        get.start()
    for get, put in moves:
        get.wait()
        put.start()
    for _, put in moves:
        put.wait()


def shards(sizes, features, history, weights, tile_values, tile_rows, tile_cols, tile_counts, span_ids):
    sections, vertices, feats = sizes
    spans, span_rows = span_ids.shape
    side = tile_values.shape[2]
    owned, width = features.shape
    rows_whole = span_rows * vertices
    rows_all = spans * span_rows
    vmem = pl.BlockSpec(memory_space=pltpu.VMEM)
    smem = pl.BlockSpec(memory_space=pltpu.SMEM)
    anywhere = pl.BlockSpec(memory_space=pl.ANY)

    dense = pl.pallas_call(
        prepare,
        name="prepare",
        out_shape=jax.ShapeDtypeStruct((spans, rows_whole, owned), jnp.bfloat16),
        in_specs=[smem, smem, smem, vmem],
        out_specs=anywhere,
        scratch_shapes=[
            pltpu.VMEM((spans, rows_whole, owned), jnp.bfloat16),
            pltpu.SemaphoreType.DMA((spans,)),
        ],
        compiler_params=pltpu.CompilerParams(vmem_limit_bytes=VMEM_BYTES),
    )(tile_rows, tile_cols, tile_counts.reshape(1, spans), tile_values)

    rows_type = jax.ShapeDtypeStruct((spans, span_rows, width), jnp.bfloat16)
    table_type = jax.ShapeDtypeStruct((owned, width), jnp.bfloat16)
    block = pltpu.VMEM(rows_type.shape, jnp.bfloat16)
    halves = 2
    pair = pltpu.SemaphoreType.DMA((spans, halves))
    layer_rows, table_new = pl.pallas_call(
        functools.partial(relay, sections, vertices, feats),
        name="relay",
        out_shape=(rows_type, table_type),
        in_specs=[anywhere, vmem, anywhere, anywhere, anywhere],
        out_specs=(vmem, anywhere),
        scratch_shapes=[
            pltpu.VMEM((min(2, spans), rows_whole, owned), jnp.bfloat16),
            pltpu.VMEM((spans, rows_whole, width), jnp.float32),
            pltpu.VMEM((spans, rows_whole, rows_all), jnp.bfloat16),
            pltpu.VMEM(weights.shape[1:], weights.dtype),
            pltpu.VMEM((owned, width), jnp.bfloat16),
            pltpu.VMEM((owned, width), jnp.bfloat16),
            pltpu.VMEM((owned, rows_all), jnp.bfloat16),
            pltpu.VMEM((rows_all, width), jnp.bfloat16),
            pltpu.VMEM((rows_all, width), jnp.bfloat16),
            block,
            pltpu.VMEM((spans, rows_whole, width), jnp.bfloat16),
            pltpu.VMEM((spans, vertices - 1, span_rows, width), jnp.bfloat16),
            block, block, block, block,
            pltpu.SemaphoreType.DMA((spans + 3,)),
            pltpu.SemaphoreType.DMA,
            pair, pair,
            pltpu.SemaphoreType.DMA((spans, vertices - 1, halves)),
            pltpu.SemaphoreType.DMA((spans, vertices - 1, halves)),
            pair, pair, pair, pair,
        ],
        compiler_params=pltpu.CompilerParams(
            vmem_limit_bytes=VMEM_BYTES, collective_id=0, has_side_effects=True
        ),
    )(dense, span_ids, weights[0], history[0], features)

    chunks = 8
    layer_rows, table_new = pl.pallas_call(
        deliver,
        name="deliver",
        out_shape=(rows_type, table_type),
        in_specs=[anywhere, anywhere],
        out_specs=(anywhere, anywhere),
        scratch_shapes=[
            block,
            pltpu.VMEM(table_type.shape, jnp.bfloat16),
            pltpu.SemaphoreType.DMA((chunks + 1,)),
            pltpu.SemaphoreType.DMA((chunks + 1,)),
        ],
        compiler_params=pltpu.CompilerParams(vmem_limit_bytes=VMEM_BYTES),
    )(layer_rows, table_new)
    return (layer_rows[None], table_new[None])


def solution(mesh):
    placed = (
        P("vertex", "feat"),
        P("section", "vertex", "feat"),
        P("section", None, "feat"),
        P(None, "vertex", None, None),
        P(None, "vertex"),
        P(None, "vertex"),
        P(None, "vertex"),
        P(None, "vertex"),
    )
    sizes = (mesh.shape["section"], mesh.shape["vertex"], mesh.shape["feat"])
    return jax.shard_map(
        functools.partial(shards, sizes),
        mesh=mesh,
        in_specs=placed,
        out_specs=(P("section", None, "vertex", "feat"), P("section", "vertex", "feat")),
        check_vma=False,
    )
```

```python
import functools

import jax
import jax.numpy as jnp
from jax import lax
from jax.experimental import pallas as pl
from jax.experimental.pallas import tpu as pltpu
from jax.sharding import PartitionSpec as P

RESIDUAL_SHARE = 0.2
BETA_SCALE = 0.5
MESH = pl.DeviceIdType.MESH
VMEM_BYTES = 60_000 * 1024


def chosen(ids_row, rows, first=0):
    shape = (rows, ids_row.shape[1])
    return (lax.broadcasted_iota(jnp.int32, shape, 0) + first == ids_row).astype(jnp.float32)


def prepare(rows_ref, cols_ref, counts_ref, tiles_ref, dense_hbm, dense, dense_sem):
    spans, _, side, _ = tiles_ref.shape
    copies = []
    for span in range(spans):
        dense[span] = jnp.zeros(dense.shape[1:], dense.dtype)

        def place(t, _, span=span):
            row = pl.multiple_of(rows_ref[span, t] * side, side)
            col = pl.multiple_of(cols_ref[span, t] * side, side)
            dense[span, pl.ds(row, side), pl.ds(col, side)] = tiles_ref[span, t]
            return 0

        lax.fori_loop(0, counts_ref[0, span], place, 0)
        copies.append(pltpu.make_async_copy(dense.at[span], dense_hbm.at[span], dense_sem.at[span]))
        copies[-1].start()
    for copy in copies:
        copy.wait()


def relay(
    sections, vertices, feats,
    dense_hbm, ids_ref, weight_hbm, kept_hbm, features_hbm, out_ref, table_hbm,
    dense, base_ref, picks_ref, weight_ref, kept_ref, features_ref, select_ref, initial_ref, fresh_ref,
    arrived, partial, parts, passing, support, other, result,
    load_sem, table_sem, x_send, x_recv, p_send, p_recv, h_send, h_recv, s_send, s_recv,
):
    section = lax.axis_index("section")
    vertex = lax.axis_index("vertex")
    feat = lax.axis_index("feat")
    spans, span_rows, width = arrived.shape
    last = vertices - 1
    partner = lax.rem(feat + 1, feats)
    beta = jnp.log(BETA_SCALE / (section + 1).astype(jnp.float32) + 1.0)
    halves = 2
    piece = span_rows // halves
    relayed = vertices > 3

    rows_whole = dense.shape[1]
    owned = kept_ref.shape[0]
    group = min(512, rows_whole)
    chunk = min(256, owned)

    def load_dense(span):
        return pltpu.make_async_copy(dense_hbm.at[span], dense.at[span % 2], load_sem.at[span])

    load_weight = pltpu.make_async_copy(weight_hbm, weight_ref, load_sem.at[spans])
    load_kept = pltpu.make_async_copy(kept_hbm, kept_ref, load_sem.at[spans + 1])
    load_features = pltpu.make_async_copy(features_hbm, features_ref, load_sem.at[spans + 2])
    load_kept.start()
    load_features.start()
    for span in range(min(2, spans)):
        load_dense(span).start()
    load_weight.start()

    barrier = pltpu.get_barrier_semaphore()
    for step in range(1, vertices):
        peer = lax.rem(vertex + step, vertices)
        pl.semaphore_signal(barrier, inc=1, device_id=(section, peer, feat), device_id_type=MESH)
    pl.semaphore_signal(barrier, inc=1, device_id=(section, vertex, partner), device_id_type=MESH)
    for step in (1, sections - 1):
        peer = lax.rem(section + step, sections)
        pl.semaphore_signal(barrier, inc=1, device_id=(peer, vertex, feat), device_id_type=MESH)
    if relayed:
        @pl.when(vertex == 0)
        def _():
            parts[:, 0] = jnp.zeros((spans, span_rows, width), jnp.bfloat16)

        @pl.when(vertex == last)
        def _():
            parts[:, last - 1] = jnp.zeros((spans, span_rows, width), jnp.bfloat16)

    pl.semaphore_wait(barrier, vertices - 1 + 1 + 2)

    def half_of(half):
        return slice(half * piece, (half + 1) * piece)

    def row_copy(span, half):
        rows = pl.ds(half * piece, piece)
        return pltpu.make_async_remote_copy(
            src_ref=result.at[span, rows], dst_ref=arrived.at[span, rows],
            send_sem=x_send.at[span, half], recv_sem=x_recv.at[span, half],
            device_id=(lax.rem(section + 1, sections), vertex, feat), device_id_type=MESH,
        )

    def chunk_rows(peer, half):
        return pl.ds(pl.multiple_of(peer * span_rows + half * piece, piece), piece)

    def part_copy(span, step, half):
        peer = lax.rem(vertex + step, vertices)
        return pltpu.make_async_remote_copy(
            src_ref=partial.at[span, chunk_rows(peer, half)],
            dst_ref=parts.at[span, step - 1, pl.ds(half * piece, piece)],
            send_sem=p_send.at[span, step - 1, half], recv_sem=p_recv.at[span, step - 1, half],
            device_id=(section, peer, feat), device_id_type=MESH,
        )

    def pass_copy(span, half):
        far = jnp.where(vertex == 0, last, 0)
        near = jnp.where(vertex == 0, 1, last - 1)
        return pltpu.make_async_remote_copy(
            src_ref=partial.at[span, chunk_rows(far, half)],
            dst_ref=passing.at[span, pl.ds(half * piece, piece)],
            send_sem=h_send.at[span, half], recv_sem=h_recv.at[span, half],
            device_id=(section, near, feat), device_id_type=MESH,
        )

    def support_copy(span, half):
        rows = pl.ds(half * piece, piece)
        return pltpu.make_async_remote_copy(
            src_ref=support.at[span, rows], dst_ref=other.at[span, rows],
            send_sem=s_send.at[span, half], recv_sem=s_recv.at[span, half],
            device_id=(section, vertex, partner), device_id_type=MESH,
        )

    at_end = (vertex == 0) | (vertex == last)

    def is_direct(step):
        if not relayed:
            return vertex >= 0
        peer = lax.rem(vertex + step, vertices)
        ends = ((vertex == 0) & (peer == last)) | ((vertex == last) & (peer == 0))
        inner = ((vertex == 1) & (peer == last)) | ((vertex == last - 1) & (peer == 0))
        return jnp.logical_not(ends | inner)

    def is_sent(step):
        if not relayed:
            return vertex >= 0
        peer = lax.rem(vertex + step, vertices)
        return jnp.logical_not(((vertex == 0) & (peer == last)) | ((vertex == last) & (peer == 0)))

    def is_received(step):
        if not relayed:
            return vertex >= 0
        source = lax.rem(vertex + vertices - step, vertices)
        return jnp.logical_not(((vertex == 0) & (source == last)) | ((vertex == last) & (source == 0)))

    def local(span, leading):
        mine = slice(span * span_rows, (span + 1) * span_rows)
        used = (span + 1) * span_rows

        def clear(i, _):
            first = pl.multiple_of(i * chunk, chunk)
            here = pl.ds(first, chunk)
            hot = chosen(ids_ref[span : span + 1, :], chunk, first)
            select_ref[here, mine] = hot.astype(jnp.bfloat16)
            taken = jnp.max(hot, axis=1, keepdims=True) > 0.5
            filler = features_ref[here, :].astype(jnp.float32) if leading else 0.0
            kept_ref[here, :] = jnp.where(taken, filler, kept_ref[here, :].astype(jnp.float32)).astype(jnp.bfloat16)
            return 0

        lax.fori_loop(0, owned // chunk, clear, 0)
        load_dense(span).wait()

        def multiply(i, _):
            here = pl.ds(pl.multiple_of(i * group, group), group)
            block = dense[span % 2, here, :]
            product = jnp.dot(block, kept_ref[...], preferred_element_type=jnp.float32)
            if leading:
                partial[span, here, :] = product.astype(jnp.bfloat16)
            else:
                base_ref[span, here, :] = product
                picks_ref[span, here, :used] = jnp.dot(
                    block, select_ref[:, :used], preferred_element_type=jnp.float32
                ).astype(jnp.bfloat16)
            return 0

        lax.fori_loop(0, rows_whole // group, multiply, 0)
        if span + 2 < spans:
            load_dense(span + 2).start()

    def gather():
        initial_ref[...] = lax.dot_general(
            select_ref[...], features_ref[...], (((0,), (0,)), ((), ())), preferred_element_type=jnp.float32
        ).astype(jnp.bfloat16)

    def scatter(span):
        mine = slice(span * span_rows, (span + 1) * span_rows)
        @pl.when(section > 0)
        def _():
            for half in range(halves):
                row_copy(span, half).wait_recv()
            fresh_ref[mine, :] = arrived[span]

        used = (span + 1) * span_rows

        def compute(peer):
            here = pl.ds(pl.multiple_of(peer * span_rows, span_rows), span_rows)
            total = base_ref[span, here, :] + jnp.dot(
                picks_ref[span, here, :used], fresh_ref[:used, :], preferred_element_type=jnp.float32
            )
            partial[span, here, :] = total.astype(jnp.bfloat16)

        if relayed:
            @pl.when(at_end & (section > 0))
            def _():
                compute(jnp.where(vertex == 0, last, 0))

            @pl.when(at_end)
            def _():
                for half in range(halves):
                    pass_copy(span, half).start()

        for step in range(1, vertices):
            @pl.when(is_sent(step) & (section > 0))
            def _(step=step):
                compute(lax.rem(vertex + step, vertices))

            @pl.when(is_direct(step))
            def _(step=step):
                part_copy(span, step, 0).start()

        for half in range(1, halves):
            for step in range(1, vertices):
                @pl.when(is_direct(step))
                def _(step=step, half=half):
                    part_copy(span, step, half).start()

        @pl.when(section > 0)
        def _():
            compute(vertex)

    def pass_on(span):
        if relayed:
            for who, step in ((1, last - 1), (last - 1, 2)):
                @pl.when(vertex == who)
                def _(who=who, step=step):
                    far = last if who == 1 else 0
                    for half in range(halves):
                        pass_copy(span, half).wait_recv()
                        here = pl.ds(far * span_rows + half * piece, piece)
                        partial[span, here, :] = (
                            partial[span, here, :].astype(jnp.float32)
                            + passing[span, half_of(half), :].astype(jnp.float32)
                        ).astype(jnp.bfloat16)
                        part_copy(span, step, half).start()

    def finish(span, half):
        total = partial[span, chunk_rows(vertex, half), :].astype(jnp.float32)
        for step in range(1, vertices):
            @pl.when(is_received(step))
            def _(step=step):
                part_copy(span, step, half).wait_recv()

        for step in range(1, vertices):
            total += parts[span, step - 1, half_of(half), :].astype(jnp.float32)
        mixed = (
            (1.0 - RESIDUAL_SHARE) * total
            + RESIDUAL_SHARE * initial_ref[pl.ds(span * span_rows + half * piece, piece), :].astype(jnp.float32)
        ).astype(jnp.bfloat16)
        support[span, half_of(half), :] = mixed
        support_copy(span, half).start()
        mine = pl.ds(pl.multiple_of(feat * width, width), width)
        theirs = pl.ds(pl.multiple_of(partner * width, width), width)
        projected = jnp.dot(mixed, weight_ref[mine, :], preferred_element_type=jnp.float32)
        support_copy(span, half).wait_recv()
        projected += jnp.dot(other[span, half_of(half), :], weight_ref[theirs, :], preferred_element_type=jnp.float32)
        rows = jnp.maximum((1.0 - beta) * mixed.astype(jnp.float32) + beta * projected, 0.0).astype(jnp.bfloat16)
        result[span, half_of(half), :] = rows
        out_ref[span, half_of(half), :] = rows

        @pl.when(section < sections - 1)
        def _():
            row_copy(span, half).start()

    def finish_all(span):
        for half in range(halves):
            finish(span, half)

    load_kept.wait()
    load_features.wait()

    @pl.when(section == 0)
    def _():
        for span in range(spans):
            local(span, True)
            if span:
                pass_on(span - 1)
            scatter(span)
        gather()
        load_weight.wait()
        for span in range(spans - 1):
            finish_all(span)
            if span == 0:
                pass_on(spans - 1)

    @pl.when(section > 0)
    def _():
        for span in range(spans):
            local(span, False)
        gather()
        load_weight.wait()
        for span in range(spans):
            scatter(span)
            pass_on(span)
            if span:
                finish_all(span - 1)

    def merge(i, _):
        here = pl.ds(pl.multiple_of(i * chunk, chunk), chunk)
        moved = jnp.dot(select_ref[here, :], fresh_ref[...], preferred_element_type=jnp.float32)
        kept_ref[here, :] = (kept_ref[here, :].astype(jnp.float32) + moved).astype(jnp.bfloat16)
        return 0

    @pl.when(section > 0)
    def _():
        lax.fori_loop(0, owned // chunk, merge, 0)

    store = pltpu.make_async_copy(kept_ref, table_hbm, table_sem)
    store.start()
    finish_all(spans - 1)

    for span in range(spans):
        for half in range(halves):
            support_copy(span, half).wait_send()
            for step in range(1, vertices):
                @pl.when(is_sent(step))
                def _(span=span, step=step, half=half):
                    part_copy(span, step, half).wait_send()

            if relayed:
                @pl.when(at_end)
                def _(span=span, half=half):
                    pass_copy(span, half).wait_send()

            @pl.when(section < sections - 1)
            def _(span=span, half=half):
                row_copy(span, half).wait_send()

    store.wait()


def deliver(rows_hbm, table_hbm, rows_out, table_out, rows_ref, table_ref, in_sem, out_sem):
    chunks = in_sem.shape[0] - 1
    size = table_ref.shape[0] // chunks
    moves = []
    for i in range(chunks):
        here = pl.ds(i * size, size)
        moves.append((
            pltpu.make_async_copy(table_hbm.at[here], table_ref.at[here], in_sem.at[i]),
            pltpu.make_async_copy(table_ref.at[here], table_out.at[here], out_sem.at[i]),
        ))
    moves.append((
        pltpu.make_async_copy(rows_hbm, rows_ref, in_sem.at[chunks]),
        pltpu.make_async_copy(rows_ref, rows_out, out_sem.at[chunks]),
    ))
    for get, _ in moves:
        get.start()
    for get, put in moves:
        get.wait()
        put.start()
    for _, put in moves:
        put.wait()


def shards(sizes, features, history, weights, tile_values, tile_rows, tile_cols, tile_counts, span_ids):
    sections, vertices, feats = sizes
    spans, span_rows = span_ids.shape
    side = tile_values.shape[2]
    owned, width = features.shape
    rows_whole = span_rows * vertices
    rows_all = spans * span_rows
    vmem = pl.BlockSpec(memory_space=pltpu.VMEM)
    smem = pl.BlockSpec(memory_space=pltpu.SMEM)
    anywhere = pl.BlockSpec(memory_space=pl.ANY)

    dense = pl.pallas_call(
        prepare,
        name="prepare",
        out_shape=jax.ShapeDtypeStruct((spans, rows_whole, owned), jnp.bfloat16),
        in_specs=[smem, smem, smem, vmem],
        out_specs=anywhere,
        scratch_shapes=[
            pltpu.VMEM((spans, rows_whole, owned), jnp.bfloat16),
            pltpu.SemaphoreType.DMA((spans,)),
        ],
        compiler_params=pltpu.CompilerParams(vmem_limit_bytes=VMEM_BYTES),
    )(tile_rows, tile_cols, tile_counts.reshape(1, spans), tile_values)

    rows_type = jax.ShapeDtypeStruct((spans, span_rows, width), jnp.bfloat16)
    table_type = jax.ShapeDtypeStruct((owned, width), jnp.bfloat16)
    block = pltpu.VMEM(rows_type.shape, jnp.bfloat16)
    halves = 2
    pair = pltpu.SemaphoreType.DMA((spans, halves))
    layer_rows, table_new = pl.pallas_call(
        functools.partial(relay, sections, vertices, feats),
        name="relay",
        out_shape=(rows_type, table_type),
        in_specs=[anywhere, vmem, anywhere, anywhere, anywhere],
        out_specs=(vmem, anywhere),
        scratch_shapes=[
            pltpu.VMEM((min(2, spans), rows_whole, owned), jnp.bfloat16),
            pltpu.VMEM((spans, rows_whole, width), jnp.float32),
            pltpu.VMEM((spans, rows_whole, rows_all), jnp.bfloat16),
            pltpu.VMEM(weights.shape[1:], weights.dtype),
            pltpu.VMEM((owned, width), jnp.bfloat16),
            pltpu.VMEM((owned, width), jnp.bfloat16),
            pltpu.VMEM((owned, rows_all), jnp.bfloat16),
            pltpu.VMEM((rows_all, width), jnp.bfloat16),
            pltpu.VMEM((rows_all, width), jnp.bfloat16),
            block,
            pltpu.VMEM((spans, rows_whole, width), jnp.bfloat16),
            pltpu.VMEM((spans, vertices - 1, span_rows, width), jnp.bfloat16),
            block, block, block, block,
            pltpu.SemaphoreType.DMA((spans + 3,)),
            pltpu.SemaphoreType.DMA,
            pair, pair,
            pltpu.SemaphoreType.DMA((spans, vertices - 1, halves)),
            pltpu.SemaphoreType.DMA((spans, vertices - 1, halves)),
            pair, pair, pair, pair,
        ],
        compiler_params=pltpu.CompilerParams(
            vmem_limit_bytes=VMEM_BYTES, collective_id=0, has_side_effects=True
        ),
    )(dense, span_ids, weights[0], history[0], features)

    chunks = 8
    layer_rows, table_new = pl.pallas_call(
        deliver,
        name="deliver",
        out_shape=(rows_type, table_type),
        in_specs=[anywhere, anywhere],
        out_specs=(anywhere, anywhere),
        scratch_shapes=[
            block,
            pltpu.VMEM(table_type.shape, jnp.bfloat16),
            pltpu.SemaphoreType.DMA((chunks + 1,)),
            pltpu.SemaphoreType.DMA((chunks + 1,)),
        ],
        compiler_params=pltpu.CompilerParams(vmem_limit_bytes=VMEM_BYTES),
    )(layer_rows, table_new)
    return (layer_rows[None], table_new[None])


def solution(mesh):
    placed = (
        P("vertex", "feat"),
        P("section", "vertex", "feat"),
        P("section", None, "feat"),
        P(None, "vertex", None, None),
        P(None, "vertex"),
        P(None, "vertex"),
        P(None, "vertex"),
        P(None, "vertex"),
    )
    sizes = (mesh.shape["section"], mesh.shape["vertex"], mesh.shape["feat"])
    return jax.shard_map(
        functools.partial(shards, sizes),
        mesh=mesh,
        in_specs=placed,
        out_specs=(P("section", None, "vertex", "feat"), P("section", "vertex", "feat")),
        check_vma=False,
    )
```

```python
import functools

import jax
import jax.numpy as jnp
from jax import lax
from jax.experimental import pallas as pl
from jax.experimental.pallas import tpu as pltpu
from jax.sharding import PartitionSpec as P

RESIDUAL_SHARE = 0.2
BETA_SCALE = 0.5
MESH = pl.DeviceIdType.MESH
VMEM_BYTES = 60_000 * 1024


def chosen(ids_row, rows, first=0):
    shape = (rows, ids_row.shape[1])
    return (lax.broadcasted_iota(jnp.int32, shape, 0) + first == ids_row).astype(jnp.float32)


def prepare(rows_ref, cols_ref, counts_ref, tiles_ref, dense_hbm, dense, dense_sem):
    spans, _, side, _ = tiles_ref.shape
    copies = []
    for span in range(spans):
        dense[span] = jnp.zeros(dense.shape[1:], dense.dtype)

        def place(t, _, span=span):
            row = pl.multiple_of(rows_ref[span, t] * side, side)
            col = pl.multiple_of(cols_ref[span, t] * side, side)
            dense[span, pl.ds(row, side), pl.ds(col, side)] = tiles_ref[span, t]
            return 0

        lax.fori_loop(0, counts_ref[0, span], place, 0)
        copies.append(pltpu.make_async_copy(dense.at[span], dense_hbm.at[span], dense_sem.at[span]))
        copies[-1].start()
    for copy in copies:
        copy.wait()


def relay(
    sections, vertices, feats,
    dense_hbm, ids_ref, weight_hbm, kept_hbm, features_hbm, out_ref, table_hbm,
    dense, base_ref, picks_ref, weight_ref, kept_ref, features_ref, select_ref, initial_ref, fresh_ref,
    arrived, partial, parts, passing, support, other, result,
    load_sem, table_sem, x_send, x_recv, p_send, p_recv, h_send, h_recv, s_send, s_recv,
):
    section = lax.axis_index("section")
    vertex = lax.axis_index("vertex")
    feat = lax.axis_index("feat")
    spans, span_rows, width = arrived.shape
    last = vertices - 1
    partner = lax.rem(feat + 1, feats)
    beta = jnp.log(BETA_SCALE / (section + 1).astype(jnp.float32) + 1.0)
    halves = 2
    piece = span_rows // halves
    relayed = vertices > 3

    rows_whole = dense.shape[1]
    owned = kept_ref.shape[0]
    group = min(512, rows_whole)
    chunk = min(256, owned)

    def load_dense(span):
        return pltpu.make_async_copy(dense_hbm.at[span], dense.at[span % 2], load_sem.at[span])

    load_weight = pltpu.make_async_copy(weight_hbm, weight_ref, load_sem.at[spans])
    load_kept = pltpu.make_async_copy(kept_hbm, kept_ref, load_sem.at[spans + 1])
    load_features = pltpu.make_async_copy(features_hbm, features_ref, load_sem.at[spans + 2])
    load_kept.start()
    load_features.start()
    for span in range(min(2, spans)):
        load_dense(span).start()
    load_weight.start()

    barrier = pltpu.get_barrier_semaphore()
    for step in range(1, vertices):
        peer = lax.rem(vertex + step, vertices)
        pl.semaphore_signal(barrier, inc=1, device_id=(section, peer, feat), device_id_type=MESH)
    pl.semaphore_signal(barrier, inc=1, device_id=(section, vertex, partner), device_id_type=MESH)
    for step in (1, sections - 1):
        peer = lax.rem(section + step, sections)
        pl.semaphore_signal(barrier, inc=1, device_id=(peer, vertex, feat), device_id_type=MESH)
    if relayed:
        @pl.when(vertex == 0)
        def _():
            parts[:, 0] = jnp.zeros((spans, span_rows, width), jnp.bfloat16)

        @pl.when(vertex == last)
        def _():
            parts[:, last - 1] = jnp.zeros((spans, span_rows, width), jnp.bfloat16)

    pl.semaphore_wait(barrier, vertices - 1 + 1 + 2)

    def half_of(half):
        return slice(half * piece, (half + 1) * piece)

    def row_copy(span, half):
        rows = pl.ds(half * piece, piece)
        return pltpu.make_async_remote_copy(
            src_ref=result.at[span, rows], dst_ref=arrived.at[span, rows],
            send_sem=x_send.at[span, half], recv_sem=x_recv.at[span, half],
            device_id=(lax.rem(section + 1, sections), vertex, feat), device_id_type=MESH,
        )

    def chunk_rows(peer, half):
        return pl.ds(pl.multiple_of(peer * span_rows + half * piece, piece), piece)

    def part_copy(span, step, half):
        peer = lax.rem(vertex + step, vertices)
        return pltpu.make_async_remote_copy(
            src_ref=partial.at[span, chunk_rows(peer, half)],
            dst_ref=parts.at[span, step - 1, pl.ds(half * piece, piece)],
            send_sem=p_send.at[span, step - 1, half], recv_sem=p_recv.at[span, step - 1, half],
            device_id=(section, peer, feat), device_id_type=MESH,
        )

    def pass_copy(span, half):
        far = jnp.where(vertex == 0, last, 0)
        near = jnp.where(vertex == 0, 1, last - 1)
        return pltpu.make_async_remote_copy(
            src_ref=partial.at[span, chunk_rows(far, half)],
            dst_ref=passing.at[span, pl.ds(half * piece, piece)],
            send_sem=h_send.at[span, half], recv_sem=h_recv.at[span, half],
            device_id=(section, near, feat), device_id_type=MESH,
        )

    def support_copy(span, half):
        rows = pl.ds(half * piece, piece)
        return pltpu.make_async_remote_copy(
            src_ref=support.at[span, rows], dst_ref=other.at[span, rows],
            send_sem=s_send.at[span, half], recv_sem=s_recv.at[span, half],
            device_id=(section, vertex, partner), device_id_type=MESH,
        )

    at_end = (vertex == 0) | (vertex == last)

    def is_direct(step):
        if not relayed:
            return vertex >= 0
        peer = lax.rem(vertex + step, vertices)
        ends = ((vertex == 0) & (peer == last)) | ((vertex == last) & (peer == 0))
        inner = ((vertex == 1) & (peer == last)) | ((vertex == last - 1) & (peer == 0))
        return jnp.logical_not(ends | inner)

    def is_sent(step):
        if not relayed:
            return vertex >= 0
        peer = lax.rem(vertex + step, vertices)
        return jnp.logical_not(((vertex == 0) & (peer == last)) | ((vertex == last) & (peer == 0)))

    def is_received(step):
        if not relayed:
            return vertex >= 0
        source = lax.rem(vertex + vertices - step, vertices)
        return jnp.logical_not(((vertex == 0) & (source == last)) | ((vertex == last) & (source == 0)))

    def local(span, leading):
        mine = slice(span * span_rows, (span + 1) * span_rows)
        used = (span + 1) * span_rows

        def clear(i, _):
            first = pl.multiple_of(i * chunk, chunk)
            here = pl.ds(first, chunk)
            hot = chosen(ids_ref[span : span + 1, :], chunk, first)
            select_ref[here, mine] = hot.astype(jnp.bfloat16)
            taken = jnp.max(hot, axis=1, keepdims=True) > 0.5
            filler = features_ref[here, :].astype(jnp.float32) if leading else 0.0
            kept_ref[here, :] = jnp.where(taken, filler, kept_ref[here, :].astype(jnp.float32)).astype(jnp.bfloat16)
            return 0

        lax.fori_loop(0, owned // chunk, clear, 0)
        load_dense(span).wait()

        def multiply(i, _):
            here = pl.ds(pl.multiple_of(i * group, group), group)
            block = dense[span % 2, here, :]
            product = jnp.dot(block, kept_ref[...], preferred_element_type=jnp.float32)
            if leading:
                partial[span, here, :] = product.astype(jnp.bfloat16)
            else:
                base_ref[span, here, :] = product
                picks_ref[span, here, :used] = jnp.dot(
                    block, select_ref[:, :used], preferred_element_type=jnp.float32
                ).astype(jnp.bfloat16)
            return 0

        lax.fori_loop(0, rows_whole // group, multiply, 0)
        if span + 2 < spans:
            load_dense(span + 2).start()

    def gather():
        initial_ref[...] = lax.dot_general(
            select_ref[...], features_ref[...], (((0,), (0,)), ((), ())), preferred_element_type=jnp.float32
        ).astype(jnp.bfloat16)

    def earlier(span):
        used = span * span_rows

        def add(i, _):
            here = pl.ds(pl.multiple_of(i * group, group), group)
            base_ref[span, here, :] += jnp.dot(
                picks_ref[span, here, :used], fresh_ref[:used, :], preferred_element_type=jnp.float32
            )
            return 0

        lax.fori_loop(0, rows_whole // group, add, 0)

    def scatter(span):
        mine = slice(span * span_rows, (span + 1) * span_rows)
        @pl.when(section > 0)
        def _():
            for half in range(halves):
                row_copy(span, half).wait_recv()
            fresh_ref[mine, :] = arrived[span]


        def compute(peer):
            here = pl.ds(pl.multiple_of(peer * span_rows, span_rows), span_rows)
            total = base_ref[span, here, :] + jnp.dot(
                picks_ref[span, here, mine], fresh_ref[mine, :], preferred_element_type=jnp.float32
            )
            partial[span, here, :] = total.astype(jnp.bfloat16)

        if relayed:
            @pl.when(at_end & (section > 0))
            def _():
                compute(jnp.where(vertex == 0, last, 0))

            @pl.when(at_end)
            def _():
                for half in range(halves):
                    pass_copy(span, half).start()

        for step in range(1, vertices):
            @pl.when(is_sent(step) & (section > 0))
            def _(step=step):
                compute(lax.rem(vertex + step, vertices))

            @pl.when(is_direct(step))
            def _(step=step):
                part_copy(span, step, 0).start()

        for half in range(1, halves):
            for step in range(1, vertices):
                @pl.when(is_direct(step))
                def _(step=step, half=half):
                    part_copy(span, step, half).start()

        @pl.when(section > 0)
        def _():
            compute(vertex)

    def pass_on(span):
        if relayed:
            for who, step in ((1, last - 1), (last - 1, 2)):
                @pl.when(vertex == who)
                def _(who=who, step=step):
                    far = last if who == 1 else 0
                    for half in range(halves):
                        pass_copy(span, half).wait_recv()
                        here = pl.ds(far * span_rows + half * piece, piece)
                        partial[span, here, :] = (
                            partial[span, here, :].astype(jnp.float32)
                            + passing[span, half_of(half), :].astype(jnp.float32)
                        ).astype(jnp.bfloat16)
                        part_copy(span, step, half).start()

    def finish(span, half):
        total = partial[span, chunk_rows(vertex, half), :].astype(jnp.float32)
        for step in range(1, vertices):
            @pl.when(is_received(step))
            def _(step=step):
                part_copy(span, step, half).wait_recv()

        for step in range(1, vertices):
            total += parts[span, step - 1, half_of(half), :].astype(jnp.float32)
        mixed = (
            (1.0 - RESIDUAL_SHARE) * total
            + RESIDUAL_SHARE * initial_ref[pl.ds(span * span_rows + half * piece, piece), :].astype(jnp.float32)
        ).astype(jnp.bfloat16)
        support[span, half_of(half), :] = mixed
        support_copy(span, half).start()
        mine = pl.ds(pl.multiple_of(feat * width, width), width)
        theirs = pl.ds(pl.multiple_of(partner * width, width), width)
        projected = jnp.dot(mixed, weight_ref[mine, :], preferred_element_type=jnp.float32)
        support_copy(span, half).wait_recv()
        projected += jnp.dot(other[span, half_of(half), :], weight_ref[theirs, :], preferred_element_type=jnp.float32)
        rows = jnp.maximum((1.0 - beta) * mixed.astype(jnp.float32) + beta * projected, 0.0).astype(jnp.bfloat16)
        result[span, half_of(half), :] = rows
        out_ref[span, half_of(half), :] = rows

        @pl.when(section < sections - 1)
        def _():
            row_copy(span, half).start()

    def finish_all(span):
        for half in range(halves):
            finish(span, half)

    load_kept.wait()
    load_features.wait()

    @pl.when(section == 0)
    def _():
        for span in range(spans):
            local(span, True)
            scatter(span)
            if span:
                pass_on(span - 1)
        gather()
        load_weight.wait()
        for span in range(spans - 1):
            finish_all(span)
            if span == 0:
                pass_on(spans - 1)

    @pl.when(section > 0)
    def _():
        for span in range(spans):
            local(span, False)
        gather()
        load_weight.wait()
        for span in range(spans):
            scatter(span)
            pass_on(span)
            if span:
                finish_all(span - 1)
            if span + 1 < spans:
                earlier(span + 1)

    def merge(i, _):
        here = pl.ds(pl.multiple_of(i * chunk, chunk), chunk)
        moved = jnp.dot(select_ref[here, :], fresh_ref[...], preferred_element_type=jnp.float32)
        kept_ref[here, :] = (kept_ref[here, :].astype(jnp.float32) + moved).astype(jnp.bfloat16)
        return 0

    @pl.when(section > 0)
    def _():
        lax.fori_loop(0, owned // chunk, merge, 0)

    store = pltpu.make_async_copy(kept_ref, table_hbm, table_sem)
    store.start()
    finish_all(spans - 1)

    for span in range(spans):
        for half in range(halves):
            support_copy(span, half).wait_send()
            for step in range(1, vertices):
                @pl.when(is_sent(step))
                def _(span=span, step=step, half=half):
                    part_copy(span, step, half).wait_send()

            if relayed:
                @pl.when(at_end)
                def _(span=span, half=half):
                    pass_copy(span, half).wait_send()

            @pl.when(section < sections - 1)
            def _(span=span, half=half):
                row_copy(span, half).wait_send()

    store.wait()


def deliver(rows_hbm, table_hbm, rows_out, table_out, rows_ref, table_ref, in_sem, out_sem):
    chunks = in_sem.shape[0] - 1
    size = table_ref.shape[0] // chunks
    moves = []
    for i in range(chunks):
        here = pl.ds(i * size, size)
        moves.append((
            pltpu.make_async_copy(table_hbm.at[here], table_ref.at[here], in_sem.at[i]),
            pltpu.make_async_copy(table_ref.at[here], table_out.at[here], out_sem.at[i]),
        ))
    moves.append((
        pltpu.make_async_copy(rows_hbm, rows_ref, in_sem.at[chunks]),
        pltpu.make_async_copy(rows_ref, rows_out, out_sem.at[chunks]),
    ))
    for get, _ in moves:
        get.start()
    for get, put in moves:
        get.wait()
        put.start()
    for _, put in moves:
        put.wait()


def shards(sizes, features, history, weights, tile_values, tile_rows, tile_cols, tile_counts, span_ids):
    sections, vertices, feats = sizes
    spans, span_rows = span_ids.shape
    side = tile_values.shape[2]
    owned, width = features.shape
    rows_whole = span_rows * vertices
    rows_all = spans * span_rows
    vmem = pl.BlockSpec(memory_space=pltpu.VMEM)
    smem = pl.BlockSpec(memory_space=pltpu.SMEM)
    anywhere = pl.BlockSpec(memory_space=pl.ANY)

    dense = pl.pallas_call(
        prepare,
        name="prepare",
        out_shape=jax.ShapeDtypeStruct((spans, rows_whole, owned), jnp.bfloat16),
        in_specs=[smem, smem, smem, vmem],
        out_specs=anywhere,
        scratch_shapes=[
            pltpu.VMEM((spans, rows_whole, owned), jnp.bfloat16),
            pltpu.SemaphoreType.DMA((spans,)),
        ],
        compiler_params=pltpu.CompilerParams(vmem_limit_bytes=VMEM_BYTES),
    )(tile_rows, tile_cols, tile_counts.reshape(1, spans), tile_values)

    rows_type = jax.ShapeDtypeStruct((spans, span_rows, width), jnp.bfloat16)
    table_type = jax.ShapeDtypeStruct((owned, width), jnp.bfloat16)
    block = pltpu.VMEM(rows_type.shape, jnp.bfloat16)
    halves = 2
    pair = pltpu.SemaphoreType.DMA((spans, halves))
    layer_rows, table_new = pl.pallas_call(
        functools.partial(relay, sections, vertices, feats),
        name="relay",
        out_shape=(rows_type, table_type),
        in_specs=[anywhere, vmem, anywhere, anywhere, anywhere],
        out_specs=(vmem, anywhere),
        scratch_shapes=[
            pltpu.VMEM((min(2, spans), rows_whole, owned), jnp.bfloat16),
            pltpu.VMEM((spans, rows_whole, width), jnp.float32),
            pltpu.VMEM((spans, rows_whole, rows_all), jnp.bfloat16),
            pltpu.VMEM(weights.shape[1:], weights.dtype),
            pltpu.VMEM((owned, width), jnp.bfloat16),
            pltpu.VMEM((owned, width), jnp.bfloat16),
            pltpu.VMEM((owned, rows_all), jnp.bfloat16),
            pltpu.VMEM((rows_all, width), jnp.bfloat16),
            pltpu.VMEM((rows_all, width), jnp.bfloat16),
            block,
            pltpu.VMEM((spans, rows_whole, width), jnp.bfloat16),
            pltpu.VMEM((spans, vertices - 1, span_rows, width), jnp.bfloat16),
            block, block, block, block,
            pltpu.SemaphoreType.DMA((spans + 3,)),
            pltpu.SemaphoreType.DMA,
            pair, pair,
            pltpu.SemaphoreType.DMA((spans, vertices - 1, halves)),
            pltpu.SemaphoreType.DMA((spans, vertices - 1, halves)),
            pair, pair, pair, pair,
        ],
        compiler_params=pltpu.CompilerParams(
            vmem_limit_bytes=VMEM_BYTES, collective_id=0, has_side_effects=True
        ),
    )(dense, span_ids, weights[0], history[0], features)

    chunks = 8
    layer_rows, table_new = pl.pallas_call(
        deliver,
        name="deliver",
        out_shape=(rows_type, table_type),
        in_specs=[anywhere, anywhere],
        out_specs=(anywhere, anywhere),
        scratch_shapes=[
            block,
            pltpu.VMEM(table_type.shape, jnp.bfloat16),
            pltpu.SemaphoreType.DMA((chunks + 1,)),
            pltpu.SemaphoreType.DMA((chunks + 1,)),
        ],
        compiler_params=pltpu.CompilerParams(vmem_limit_bytes=VMEM_BYTES),
    )(layer_rows, table_new)
    return (layer_rows[None], table_new[None])


def solution(mesh):
    placed = (
        P("vertex", "feat"),
        P("section", "vertex", "feat"),
        P("section", None, "feat"),
        P(None, "vertex", None, None),
        P(None, "vertex"),
        P(None, "vertex"),
        P(None, "vertex"),
        P(None, "vertex"),
    )
    sizes = (mesh.shape["section"], mesh.shape["vertex"], mesh.shape["feat"])
    return jax.shard_map(
        functools.partial(shards, sizes),
        mesh=mesh,
        in_specs=placed,
        out_specs=(P("section", None, "vertex", "feat"), P("section", "vertex", "feat")),
        check_vma=False,
    )
```
